128 devices in a mesh: blk: 16 (over y_hi, x, core), tp: 8 (over z, y_lo).
Axes of the slice: x: 4, y: 4 (y_hi: 2, y_lo: 2; y = y_hi * 2 + y_lo), z: 4, core: 2. Of those that a mesh axis runs over, the one named last changes fastest.
Arguments:
- text_emb: bfloat16 [49152, 1024], P('blk', 'tp'), may hold values from -4 to 4
- image_emb: bfloat16 [49152, 1024], P(('blk', 'tp')), may hold values from -4 to 4
- logit_scale: float32 [1], replicated, may hold values from 4 to 12
- logit_bias: float32 [1], replicated, may hold values from -3 to -1
- bucket: int32 [49152], replicated, may hold values from 0 to 3
- positive: int32 [49152], replicated, may hold values from 0 to 49151, as said below
- blocks: int32 [384, 16, 3], replicated, may hold values from -1 to 2, as said below
Outputs:
- text_grad: bfloat16 [49152, 1024], P('blk', 'tp')
- image_grad: bfloat16 [49152, 1024], P(('blk', 'tp'))
The draws below stay inside these ranges and needn't reach their ends.
Inputs may be any that keep to these rules, and one draw needn't show every extreme that they name: positive[i] lies in the same 128-row tile as i, and within each tile the entries are a permutation of that tile's rows. `blocks`: each entry is a tile of the named shard or -1 for an unused slot; slot 0 is never -1; the used slots of one text tile and shard name different tiles; for the text tile's own blk index, slot 0 names the text tile's own tile.
All inputs are finite; a program needn't handle non-finite values.
Results may differ from the reference program's by a relative error of at most 0.015.
Values may be sent and summed in bfloat16 or wider, within the bound.
A program may use at most 128 MiB of HBM per device.

```python
import math
import jax
import jax.numpy as jnp
from jax import lax

E = 1024
TILE = 128
TILE_DEV = 3
SLOTS = 3
BUCKETS = 4
SHARDS = 16
GROUPS = 8
N = 49152
TILES = 384


def embed_draw(key_value):
    first, second, third = jax.random.split(key_value, 3)
    row_scale = jnp.exp(jax.random.uniform(first, (N, 1), jnp.float32) * math.log(10.0))
    col_scale = jnp.exp(jax.random.uniform(second, (1, E), jnp.float32) * math.log(10.0))
    base_values = jnp.clip(jax.random.normal(third, (N, E), jnp.float32), -4.0, 4.0)
    return 0.01 * row_scale * col_scale * base_values


def draw_text_emb(key, part):
    return embed_draw(jax.random.fold_in(key, 11)).astype(jnp.bfloat16)


def draw_image_emb(key, part):
    return embed_draw(jax.random.fold_in(key, 23)).astype(jnp.bfloat16)


def draw_positive(key, part):
    scores = jax.random.randint(jax.random.fold_in(key, 31), (TILES, TILE), 0, 65536) * TILE + jnp.arange(TILE, dtype=jnp.int32)[None, :]
    within = jnp.argsort(scores, axis=1, stable=True).astype(jnp.int32)
    return (jnp.arange(TILES, dtype=jnp.int32)[:, None] * TILE + within).reshape(-1).astype(jnp.int32)


def draw_blocks(key, part):
    first, second, third, fourth = jax.random.split(jax.random.fold_in(key, 37), 4)
    scores = jax.random.randint(first, (TILES, SHARDS, TILE_DEV), 0, 65536) * TILE_DEV + jnp.arange(TILE_DEV, dtype=jnp.int32)
    listing = jnp.argsort(scores, axis=-1, stable=True)[..., :SLOTS].astype(jnp.int32)
    others = jax.random.randint(second, (TILES, TILE_DEV - 1), 0, 65536) * TILE_DEV + jnp.arange(TILE_DEV - 1, dtype=jnp.int32)
    other_order = jnp.argsort(others, axis=-1, stable=True).astype(jnp.int32) + 1
    tile_ids = jnp.arange(TILES, dtype=jnp.int32)
    device_ids = tile_ids // TILE_DEV
    own_shard = device_ids // GROUPS
    own_tile = tile_ids % TILE_DEV
    offsets = jnp.concatenate([jnp.zeros((TILES, 1), jnp.int32), other_order[:, :SLOTS - 1]], axis=1)
    own_list = (own_tile[:, None] + offsets) % TILE_DEV
    is_own = jnp.arange(SHARDS, dtype=jnp.int32)[None, :] == own_shard[:, None]
    listing = jnp.where(is_own[:, :, None], own_list[:, None, :], listing)
    levels = jax.random.randint(third, (SHARDS * GROUPS,), 0, 5)[device_ids]
    live_mask = jax.random.randint(fourth, (TILES, SHARDS, SLOTS), 0, 4) < levels[:, None, None]
    live_mask = jnp.logical_or(live_mask, (jnp.arange(SLOTS, dtype=jnp.int32) == 0)[None, None, :])
    return jnp.where(live_mask, listing, -1).astype(jnp.int32)


def place_ends(result, key, low, top_value):
    longest = result.shape.index(max(result.shape))
    spots = []
    for shift in (0, 1):
        where = [jax.random.randint(jax.random.fold_in(key, axis), (), 0, length) for axis, length in enumerate(result.shape)]
        where[longest] = (where[longest] + shift) % result.shape[longest]
        spots.append(tuple(where))
    return result.at[spots[0]].set(low).at[spots[1]].set(top_value)


def setup_inputs(seed: int = 0) -> dict:
    keys = jax.random.split(jax.random.key(seed), 8)
    text_emb = draw_text_emb(jax.random.fold_in(keys[7], 71), 0)
    image_emb = draw_image_emb(jax.random.fold_in(keys[7], 71), 0)
    logit_scale = jnp.clip(jnp.exp(jax.random.uniform(keys[2], (1,), jnp.float32, math.log(4.0), math.log(12.0))), 4.0, 12.0)
    logit_bias = jnp.clip(jax.random.uniform(keys[3], (1,), jnp.float32, -3.0, -1.0), -3.0, -1.0)
    bucket = place_ends(jax.random.randint(keys[4], (N,), 0, BUCKETS), jax.random.fold_in(keys[4], 1), 0, BUCKETS - 1).astype(jnp.int32)
    positive = draw_positive(jax.random.fold_in(keys[7], 71), 0)
    blocks = draw_blocks(jax.random.fold_in(keys[7], 71), 0)
    return {"text_emb": text_emb, "image_emb": image_emb, "logit_scale": logit_scale, "logit_bias": logit_bias, "bucket": bucket, "positive": positive, "blocks": blocks}


def unit_rows(raw_rows):
    values = raw_rows.astype(jnp.float32)
    scales = lax.rsqrt(lax.optimization_barrier(jnp.sum(values * values, axis=-1, keepdims=True)) + 1e-06)
    return (values * scales, scales)

def grad_rows(raw_rows, scales, upstream):
    unit_float = raw_rows.astype(jnp.float32) * scales
    return (scales * (upstream - unit_float * lax.optimization_barrier(jnp.sum(unit_float * upstream, axis=-1, keepdims=True)))).astype(jnp.bfloat16)

def pair_weights(text_part, text_ids, image_part, image_ids, live_mask, scale_value, bias_value, positive, bucket):
    products = jnp.einsum('cid,cjd->cij', text_part.astype(jnp.float32), image_part.astype(jnp.float32))
    logits = scale_value * products + bias_value
    columns = image_ids[:, None] * TILE + jnp.arange(TILE, dtype=jnp.int32)[None, :]
    row_positive = positive.reshape(-1, TILE)[text_ids]
    row_bucket = bucket.reshape(-1, TILE)[text_ids]
    col_bucket = bucket.reshape(-1, TILE)[image_ids]
    matched = row_positive[:, :, None] == columns[:, None, :]
    labels = jnp.where(matched, 1.0, -1.0).astype(jnp.float32)
    kept_pairs = jnp.logical_or(matched, row_bucket[:, :, None] == col_bucket[:, None, :])
    pair_mask = jnp.where(kept_pairs, 1.0, 0.0).astype(jnp.float32) * jnp.where(live_mask, 1.0, 0.0).astype(jnp.float32)[:, None, None]
    return (scale_value * pair_mask * -labels * jax.nn.sigmoid(-labels * logits)).astype(jnp.bfloat16)

def reference(text_emb, image_emb, logit_scale, logit_bias, bucket, positive, blocks):
    text_float, text_scales = unit_rows(text_emb)
    image_float, image_scales = unit_rows(image_emb)
    text_unit = text_float.astype(jnp.bfloat16)
    image_unit = image_float.astype(jnp.bfloat16)
    image_tiles = image_unit.reshape(TILES, TILE, E)
    scale_value = logit_scale[0]
    bias_value = logit_bias[0]
    shard_base = jnp.arange(SHARDS, dtype=jnp.int32)[:, None] * GROUPS

    def per_tile(image_acc, tile_index):
        group = tile_index // TILE_DEV % GROUPS
        listed = lax.dynamic_index_in_dim(blocks, tile_index, 0, keepdims=False)
        live_mask = (listed >= 0).reshape(-1)
        image_ids = ((shard_base + group) * TILE_DEV + jnp.maximum(listed, 0)).reshape(-1).astype(jnp.int32)
        chosen = image_tiles[image_ids]
        text_part = lax.dynamic_slice_in_dim(text_unit, (tile_index * TILE).astype(jnp.int32), TILE, 0)
        text_rep = jnp.broadcast_to(text_part[None], (SHARDS * SLOTS, TILE, E))
        text_ids = jnp.full((SHARDS * SLOTS,), tile_index, dtype=jnp.int32)
        weights = pair_weights(text_rep, text_ids, chosen, image_ids, live_mask, scale_value, bias_value, positive, bucket)
        text_update = jnp.einsum('cij,cjd->id', weights.astype(jnp.float32), chosen.astype(jnp.float32))
        image_update = jnp.einsum('cij,id->cjd', weights.astype(jnp.float32), text_part.astype(jnp.float32))
        image_acc = image_acc.at[image_ids].add(image_update)
        return (image_acc, text_update)
    image_acc, text_acc = lax.scan(per_tile, jnp.zeros((TILES, TILE, E), jnp.float32), jnp.arange(TILES, dtype=jnp.int32))
    text_grad = grad_rows(text_emb, text_scales, text_acc.reshape(N, E))
    image_grad = grad_rows(image_emb, image_scales, image_acc.reshape(N, E))
    return (text_grad, image_grad)
```

```python
import jax
import jax.numpy as jnp
from jax import lax
from jax.experimental import pallas as pl
from jax.experimental.pallas import tpu as pltpu
from jax.sharding import PartitionSpec as P

MESH = pl.DeviceIdType.MESH
F32 = jnp.float32
BF16 = jnp.bfloat16
TILE = 128
TILES = 3
SLOTS = 3
ROWS = TILE * TILES
HALF = ROWS // 2
E = 1024
GROUPS = 8
EB = E // GROUPS
LOG2E = 1.4426950408889634
NT = (((1,), (1,)), ((), ()))
NN = (((1,), (0,)), ((), ()))
TN = (((0,), (0,)), ((), ()))


def kernel(
    scale_ref, bias_ref, text_hbm, image_hbm, bucket_hbm, positive_hbm, blocks_hbm,
    tgrad_hbm, igrad_hbm,
    traw, iraw, bucket_v, positive_v, blocks_v,
    T, I, W, rowb, cnt, trs, irs,
    tacc, lacc, iacc, send_t, send_y, send_x, got_c0, got_c1, got_y, got_l, got_r,
    relay_l, relay_r, gbuf, gimg,
    loc_sem, a2a_s, a2a_r, xs, xr, xfs, xfr, cs, cr, ys, yr, fs, fr,
    c0s, c0r, c1s, c1r, y2s, y2r, x2s, x2r, o_s, o_r,
):
    blk = lax.axis_index("blk")
    tp = lax.axis_index("tp")
    yh = blk // 8
    x = (blk // 2) % 4
    c = blk % 2
    core_dev = (blk + 1 - 2 * c, tp)
    yh_blk = (blk + 8) % 16
    y_dev = (yh_blk, tp)
    right = ((yh * 4 + (x + 1) % 4) * 2 + c, tp)
    left = ((yh * 4 + (x + 3) % 4) * 2 + c, tp)
    far_blk = (yh * 4 + (x + 2) % 4) * 2 + c
    image_blk = (blk, left[0], right[0], far_blk)
    text_blk = (blk, core_dev[0], yh_blk, yh_blk + 1 - 2 * c)

    def remote(src, dst, ssem, rsem, dev):
        return pltpu.make_async_remote_copy(
            src_ref=src, dst_ref=dst, send_sem=ssem, recv_sem=rsem,
            device_id=dev, device_id_type=MESH,
        )

    local = [
        pltpu.make_async_copy(image_hbm, iraw, loc_sem.at[0]),
        pltpu.make_async_copy(bucket_hbm, bucket_v, loc_sem.at[1]),
        pltpu.make_async_copy(positive_hbm, positive_v, loc_sem.at[2]),
    ]
    local.append(pltpu.make_async_copy(blocks_hbm, blocks_v, loc_sem.at[3]))
    own_text = pltpu.make_async_copy(
        text_hbm.at[pl.ds(pl.multiple_of(tp * ROWS, ROWS), ROWS)], traw.at[tp], loc_sem.at[7]
    )
    for cp in local:
        cp.start()
    own_text.start()

    barrier = pltpu.get_barrier_semaphore()
    peers = [(blk, (tp + k) % GROUPS) for k in range(1, GROUPS)]
    peers += [core_dev, y_dev, right, left]
    for dev in peers:
        pl.semaphore_signal(barrier, inc=1, device_id=dev, device_id_type=MESH)
    pl.semaphore_wait(barrier, len(peers))

    a2a = []
    for j in range(TILES):
        row = []
        for k in range(1, GROUPS):
            to = (tp + k) % GROUPS
            start = pl.multiple_of(to * ROWS + j * TILE, TILE)
            cp = remote(
                text_hbm.at[pl.ds(start, TILE)],
                traw.at[tp, pl.ds(j * TILE, TILE)],
                a2a_s.at[j, k - 1], a2a_r.at[j, k - 1], (blk, to),
            )
            cp.start()
            row.append(cp)
        a2a.append(row)

    local[0].wait()

    def image_half(h):
        rows = pl.ds(h * HALF, HALF)
        v = iraw[rows, :].astype(F32)
        r = lax.rsqrt(jnp.sum(v * v, axis=-1, keepdims=True) + 1e-6)
        irs[rows, :] = r
        I[rows, :] = (v * r).astype(BF16)

    def image_send(h, side):
        dev = right if side == 0 else left
        return remote(
            I.at[pl.ds(h * HALF, HALF)],
            I.at[pl.ds((1 + side) * ROWS + h * HALF, HALF)],
            xs.at[side, h], xr.at[side, h], dev,
        )

    ring = {(h, s): image_send(h, s) for h in range(2) for s in range(2)}
    image_half(0)
    ring[0, 0].start()
    image_half(1)
    ring[1, 1].start()
    ring[1, 0].start()
    ring[0, 1].start()

    scale = scale_ref[0]
    bias = bias_ref[0]
    ea = -scale * LOG2E
    eb = -bias * LOG2E
    for cp in local[1:]:
        cp.wait()

    def spread(row):
        return jnp.broadcast_to(row.astype(F32), (TILE, TILE)).T

    for s in range(4):
        def prep(j, carry, s=s):
            r = (text_blk[s] * GROUPS + tp) * TILES + j
            block = j + (TILES if s >= 2 else 0)
            rowb[block, pl.ds((s % 2) * TILE, TILE), :] = spread(bucket_v[pl.ds(r, 1), :])
            lanes = lax.broadcasted_iota(jnp.int32, blocks_v.shape[1:], 1)
            for l in range(TILES):
                n = sum(jnp.where(blocks_v[m] == l, 1.0, 0.0) for m in range(SLOTS))
                n = jnp.sum(jnp.where(lanes == r, n, 0.0), axis=1, keepdims=True)
                cnt[2 * block + s % 2, l] = jnp.broadcast_to(n * scale, (blocks_v.shape[1], TILE))
            return carry

        lax.fori_loop(0, TILES, prep, 0)

    own_text.wait()
    to_core, to_y, fwd_y = [], [], []
    for j in range(TILES):
        to_core.append(remote(T.at[j, pl.ds(0, TILE)], T.at[j, pl.ds(TILE, TILE)], cs.at[j], cr.at[j], core_dev))
        to_y.append(remote(T.at[j, pl.ds(0, TILE)], T.at[TILES + j, pl.ds(0, TILE)], ys.at[j], yr.at[j], y_dev))
        fwd_y.append(
            remote(T.at[TILES + j, pl.ds(0, TILE)], T.at[TILES + j, pl.ds(TILE, TILE)], fs.at[j], fr.at[j], core_dev)
        )

    def text_tile(j):
        for cp in a2a[j]:
            cp.wait_recv()
        rows = pl.ds(j * TILE, TILE)
        total = jnp.zeros((TILE, 1), F32)
        sq = jnp.zeros((TILE, EB), F32)
        for g in range(GROUPS):
            v = traw[g, rows, :].astype(F32)
            sq = sq + v * v
        total = jnp.sum(sq, axis=-1, keepdims=True)
        r = lax.rsqrt(total + 1e-6)
        trs[rows, :] = r
        for g in range(GROUPS):
            T[j, 0:TILE, g * EB : (g + 1) * EB] = (traw[g, rows, :].astype(F32) * r).astype(BF16)
        to_core[j].start()
        to_y[j].start()

    text_tile(0)
    text_tile(1)
    on_right = remote(
        I.at[pl.ds(ROWS, HALF)], I.at[pl.ds(3 * ROWS, HALF)], xfs.at[0], xfr.at[0], right
    )
    on_left = remote(
        I.at[pl.ds(2 * ROWS + HALF, HALF)], I.at[pl.ds(3 * ROWS + HALF, HALF)],
        xfs.at[1], xfr.at[1], left,
    )
    ring[0, 0].wait_recv()
    on_right.start()
    ring[1, 1].wait_recv()
    on_left.start()
    text_tile(2)

    def weights(lo, hi, k0, nk):
        cols = pl.ds(k0 * ROWS, nk * ROWS)

        def body(b, carry):
            s = lax.dot_general(T[b], I[cols, :], NT, preferred_element_type=F32)
            d = 1.0 + jnp.exp2(s * ea + eb)
            for h in range(2):
                rb = rowb[b, pl.ds(h * TILE, TILE), :]
                for k in range(nk):
                    shard = image_blk[k0 + k]
                    for l in range(TILES):
                        tile = (shard * GROUPS + tp) * TILES + l
                        cb = bucket_v[pl.ds(tile, 1), :].astype(F32)
                        co = cnt[2 * b + h, l, pl.ds(shard, 1), :]
                        at = (k * TILES + l) * TILE
                        dd = d[h * TILE : (h + 1) * TILE, at : at + TILE]
                        w = jnp.where(rb == cb, co, 0.0) / dd
                        W[b, pl.ds(h * TILE, TILE), pl.ds(k0 * ROWS + at, TILE)] = w.astype(BF16)
            return carry

        lax.fori_loop(lo, hi, body, 0)

    def own_pairs():
        def body(j, carry):
            at = pl.multiple_of(j * TILE, TILE)
            s = lax.dot_general(
                T[j, 0:TILE, :], I[pl.ds(at, TILE), :], NT, preferred_element_type=F32
            )
            e = jnp.exp2(s * ea + eb)
            tile = (blk * GROUPS + tp) * TILES + j
            rb = rowb[j, 0:TILE, :]
            cb = bucket_v[pl.ds(tile, 1), :].astype(F32)
            co = cnt[2 * j, j, pl.ds(blk, 1), :]
            pos = spread(positive_v[pl.ds(tile, 1), :] - tile * TILE)
            matched = pos == lax.broadcasted_iota(jnp.int32, (TILE, TILE), 1).astype(F32)
            num = jnp.where(matched, -co * e, jnp.where(rb == cb, co, 0.0))
            W[j, 0:TILE, pl.ds(at, TILE)] = (num / (1.0 + e)).astype(BF16)
            return carry

        lax.fori_loop(0, TILES, body, 0)

    for cp in to_core:
        cp.wait_recv()
    weights(0, 3, 0, 1)
    own_pairs()
    to_y[0].wait_recv()
    fwd_y[0].start()
    ring[1, 0].wait_recv()
    ring[0, 1].wait_recv()
    weights(0, 3, 1, 2)
    to_y[1].wait_recv()
    fwd_y[1].start()
    fwd_y[0].wait_recv()
    weights(3, 4, 0, 3)
    to_y[2].wait_recv()
    fwd_y[2].start()
    fwd_y[1].wait_recv()
    weights(4, 5, 0, 3)
    fwd_y[2].wait_recv()
    weights(5, 6, 0, 3)
    on_right.wait_recv()
    on_left.wait_recv()
    weights(0, 6, 3, 1)

    c1 = [
        remote(send_t.at[1, pl.ds(j * TILE, TILE)], got_c1.at[pl.ds(j * TILE, TILE)], c1s.at[j], c1r.at[j], core_dev)
        for j in range(TILES)
    ]
    c0 = [
        remote(send_t.at[0, pl.ds(j * TILE, TILE)], got_c0.at[pl.ds(j * TILE, TILE)], c0s.at[j], c0r.at[j], core_dev)
        for j in range(TILES)
    ]
    y2 = [
        remote(send_y.at[pl.ds(j * TILE, TILE)], got_y.at[pl.ds(j * TILE, TILE)], y2s.at[j], y2r.at[j], y_dev)
        for j in range(TILES)
    ]

    def text_sums(b, acc, j, which):
        u = lax.dot_general(W[b], I[...], NN, preferred_element_type=F32)
        acc[pl.ds(j * TILE, TILE), :] = u[0:TILE]
        send_t[which, pl.ds(j * TILE, TILE), :] = u[TILE:].astype(BF16)

    for j in range(TILES):
        text_sums(TILES + j, lacc, j, 1)
        c1[j].start()

    def image_sums(k):
        out = jnp.zeros((ROWS, E), F32)
        for b in range(2 * TILES):
            out = out + lax.dot_general(
                W[b, :, pl.ds(k * ROWS, ROWS)], T[b], TN, preferred_element_type=F32
            )
        return out

    first = pl.ds(0, HALF)
    second = pl.ds(HALF, HALF)
    send_x[2] = image_sums(3).astype(BF16)
    far_right = remote(send_x.at[2, first], relay_l, x2s.at[0], x2r.at[0], right)
    far_left = remote(send_x.at[2, second], relay_r, x2s.at[1], x2r.at[1], left)
    far_right.start()
    far_left.start()

    for j in range(TILES):
        rows = pl.ds(j * TILE, TILE)
        c1[j].wait_recv()
        send_y[rows, :] = (lacc[rows, :] + got_c1[rows, :].astype(F32)).astype(BF16)
        y2[j].start()

    send_x[1] = image_sums(2).astype(BF16)
    near_right = remote(send_x.at[1, second], got_l.at[second], x2s.at[2], x2r.at[2], right)
    near_right.start()
    send_x[0] = image_sums(1).astype(BF16)
    near_left = remote(send_x.at[0, first], got_r.at[first], x2s.at[3], x2r.at[3], left)
    near_left.start()

    for j in range(TILES):
        text_sums(j, tacc, j, 0)
        c0[j].start()
    iacc[...] = image_sums(0)

    far_right.wait_recv()
    send_x[1, first, :] = (send_x[1, first, :].astype(F32) + relay_l[...].astype(F32)).astype(BF16)
    sum_right = remote(send_x.at[1, first], got_l.at[first], x2s.at[4], x2r.at[4], right)
    sum_right.start()
    far_left.wait_recv()
    send_x[0, second, :] = (send_x[0, second, :].astype(F32) + relay_r[...].astype(F32)).astype(BF16)
    sum_left = remote(send_x.at[0, second], got_r.at[second], x2s.at[5], x2r.at[5], left)
    sum_left.start()

    back = []
    for j in range(TILES):
        rows = pl.ds(j * TILE, TILE)
        c0[j].wait_recv()
        y2[j].wait_recv()
        r = trs[rows, :]
        up = tacc[rows, :] + got_c0[rows, :].astype(F32) + got_y[rows, :].astype(F32)
        dot = jnp.zeros((TILE, EB), F32)
        for g in range(GROUPS):
            dot = dot + traw[g, rows, :].astype(F32) * r * up[:, g * EB : (g + 1) * EB]
        d = jnp.sum(dot, axis=-1, keepdims=True)
        for g in range(GROUPS):
            u = traw[g, rows, :].astype(F32) * r
            gbuf[g, rows, :] = (r * (up[:, g * EB : (g + 1) * EB] - u * d)).astype(BF16)
        start = pl.multiple_of(tp * ROWS + j * TILE, TILE)
        for k in range(1, GROUPS):
            to = (tp + k) % GROUPS
            cp = remote(
                gbuf.at[to, rows], tgrad_hbm.at[pl.ds(start, TILE)],
                o_s.at[j, k - 1], o_r.at[j, k - 1], (blk, to),
            )
            cp.start()
            back.append(cp)
    own_out = pltpu.make_async_copy(
        gbuf.at[tp], tgrad_hbm.at[pl.ds(pl.multiple_of(tp * ROWS, ROWS), ROWS)], loc_sem.at[8]
    )
    own_out.start()

    near_right.wait_recv()
    near_left.wait_recv()
    sum_right.wait_recv()
    sum_left.wait_recv()
    v = iraw[...].astype(F32) * irs[...]
    up = iacc[...] + got_l[...].astype(F32) + got_r[...].astype(F32)
    d = jnp.sum(v * up, axis=-1, keepdims=True)
    gimg[...] = (irs[...] * (up - v * d)).astype(BF16)
    image_out = pltpu.make_async_copy(gimg, igrad_hbm, loc_sem.at[9])
    image_out.start()

    for row in a2a:
        for cp in row:
            cp.wait_send()
    for cp in ring.values():
        cp.wait_send()
    sent = [on_right, on_left, far_right, far_left, near_right, near_left, sum_right, sum_left]
    for cp in sent + to_core + to_y + fwd_y + c0 + c1 + y2:
        cp.wait_send()
    for cp in back:
        cp.wait()
    own_out.wait()
    image_out.wait()


def per_device(text_emb, image_emb, logit_scale, logit_bias, bucket, positive, blocks):
    any_spec = pl.BlockSpec(memory_space=pl.ANY)
    smem_spec = pl.BlockSpec(memory_space=pltpu.SMEM)
    vm = pltpu.VMEM
    dma = pltpu.SemaphoreType.DMA
    tiles = bucket.shape[0] // TILE
    return pl.pallas_call(
        kernel,
        out_shape=(
            jax.ShapeDtypeStruct(text_emb.shape, BF16),
            jax.ShapeDtypeStruct(image_emb.shape, BF16),
        ),
        in_specs=[smem_spec, smem_spec] + [any_spec] * 5,
        out_specs=(any_spec, any_spec),
        scratch_shapes=[
            vm((GROUPS, ROWS, EB), BF16), vm((ROWS, E), BF16),
            vm((tiles, TILE), jnp.int32), vm((tiles, TILE), jnp.int32), vm(blocks.shape[::-1], jnp.int32),
            vm((6, 256, E), BF16), vm((4 * ROWS, E), BF16), vm((6, 256, 4 * ROWS), BF16),
            vm((6, 256, TILE), F32), vm((12, TILES, 16, TILE), F32),
            vm((ROWS, 1), F32), vm((ROWS, 1), F32),
            vm((ROWS, E), F32), vm((ROWS, E), F32), vm((ROWS, E), F32),
            vm((2, ROWS, E), BF16), vm((ROWS, E), BF16), vm((3, ROWS, E), BF16),
            vm((ROWS, E), BF16), vm((ROWS, E), BF16), vm((ROWS, E), BF16),
            vm((ROWS, E), BF16), vm((ROWS, E), BF16),
            vm((HALF, E), BF16), vm((HALF, E), BF16),
            vm((GROUPS, ROWS, EB), BF16), vm((ROWS, E), BF16),
            dma((10,)), dma((3, 7)), dma((3, 7)),
            dma((2, 2)), dma((2, 2)), dma((2,)), dma((2,)),
            dma((3,)), dma((3,)), dma((3,)), dma((3,)), dma((3,)), dma((3,)),
            dma((3,)), dma((3,)), dma((3,)), dma((3,)), dma((3,)), dma((3,)),
            dma((6,)), dma((6,)), dma((3, 7)), dma((3, 7)),
        ],
        compiler_params=pltpu.CompilerParams(
            collective_id=0, has_side_effects=True, vmem_limit_bytes=56 << 20
        ),
        name="pairs",
    )(
        logit_scale, logit_bias, text_emb, image_emb,
        bucket.reshape(tiles, TILE), positive.reshape(tiles, TILE), blocks.transpose(2, 1, 0),
    )


def solution(mesh):
    in_specs = (P("blk", "tp"), P(("blk", "tp"), None), P(), P(), P(), P(), P())
    out_specs = (P("blk", "tp"), P(("blk", "tp"), None))
    return jax.shard_map(
        per_device, mesh=mesh, in_specs=in_specs, out_specs=out_specs, check_vma=False
    )
```

```python
import jax
import jax.numpy as jnp
from jax import lax
from jax.experimental import pallas as pl
from jax.experimental.pallas import tpu as pltpu
from jax.sharding import PartitionSpec as P

MESH = pl.DeviceIdType.MESH
F32 = jnp.float32
BF16 = jnp.bfloat16
TILE = 128
TILES = 3
SLOTS = 3
ROWS = TILE * TILES
HALF = ROWS // 2
PARTS = 3
E = 1024
GROUPS = 8
EB = E // GROUPS
LOG2E = 1.4426950408889634
NT = (((1,), (1,)), ((), ()))
NN = (((1,), (0,)), ((), ()))
TN = (((0,), (0,)), ((), ()))


def kernel(
    scale_ref, bias_ref, text_hbm, image_hbm, bucket_hbm, positive_hbm, blocks_hbm,
    tgrad_out, igrad_out,
    R, pas, iraw, bucket_v, positive_v, blocks_v,
    T, I, W, rowb, cnt, trs, irs,
    tacc, iacc, pacc, send_t, send_x, got_c, got_l, got_r, relay_l, relay_r,
    keep, gsend, got_far, got_pair, got_other, gout,
    loc_sem, zs, zr, xs, xr, xfs, xfr, ys, yr, cs, cr, ps, pr, gs, gr, x2s, x2r, o_s, o_r,
):
    blk = lax.axis_index("blk")
    tp = lax.axis_index("tp")
    yh = blk // 8
    x = (blk // 2) % 4
    c = blk % 2
    z = tp // 2
    yl = tp % 2
    yh_blk = (blk + 8) % 16
    tp_pair = tp + 1 - 2 * yl
    core_dev = (blk + 1 - 2 * c, tp)
    far_y = (yh_blk, tp)
    pair_y = (blk, tp_pair)
    other_y = (yh_blk, tp_pair)
    z_devs = [(k, (blk, ((z + k) % 4) * 2 + yl)) for k in range(1, 4)]
    right = ((yh * 4 + (x + 1) % 4) * 2 + c, tp)
    left = ((yh * 4 + (x + 3) % 4) * 2 + c, tp)
    far_blk = (yh * 4 + (x + 2) % 4) * 2 + c
    image_blk = (blk, left[0], right[0], far_blk)
    text_blk = ((blk, core_dev[0]), (yh_blk, yh_blk + 1 - 2 * c))

    def remote(src, dst, ssem, rsem, dev):
        return pltpu.make_async_remote_copy(
            src_ref=src, dst_ref=dst, send_sem=ssem, recv_sem=rsem,
            device_id=dev, device_id_type=MESH,
        )

    def drain(ref, sem):
        pltpu.make_async_copy(ref, ref, sem).wait()

    local = [
        pltpu.make_async_copy(image_hbm, iraw, loc_sem.at[0]),
        pltpu.make_async_copy(bucket_hbm, bucket_v, loc_sem.at[1]),
        pltpu.make_async_copy(positive_hbm, positive_v, loc_sem.at[2]),
        pltpu.make_async_copy(blocks_hbm, blocks_v, loc_sem.at[3]),
    ]
    def own_rows(d):
        return pl.ds(pl.multiple_of((z * 2 + d) * ROWS, ROWS), ROWS)

    own_text = [
        pltpu.make_async_copy(text_hbm.at[own_rows(yl)], R.at[0, yl, z], loc_sem.at[6]),
        pltpu.make_async_copy(text_hbm.at[own_rows(1 - yl)], pas.at[z], loc_sem.at[7]),
    ]
    for cp in local:
        cp.start()
    for cp in own_text:
        cp.start()

    barrier = pltpu.get_barrier_semaphore()
    peers = [dev for _, dev in z_devs] + [far_y, pair_y, other_y, core_dev, right, left]
    for dev in peers:
        pl.semaphore_signal(barrier, inc=1, device_id=dev, device_id_type=MESH)

    local[0].wait()
    for h in range(2):
        rows = pl.ds(h * HALF, HALF)
        v = iraw[rows, :].astype(F32)
        r = lax.rsqrt(jnp.sum(v * v, axis=-1, keepdims=True) + 1e-6)
        irs[rows, :] = r
        I[rows, :] = (v * r).astype(BF16)

    pl.semaphore_wait(barrier, len(peers))

    def z_send(j):
        rows = pl.ds(j * TILE, TILE)
        for k, dev in z_devs:
            base = ((z + k) % 4) * 2
            for same in range(2):
                d = 1 - yl if same == 0 else yl
                start = pl.multiple_of((base + d) * ROWS + j * TILE, TILE)
                dst = R.at[0, yl, z, rows] if same else pas.at[z, rows]
                remote(text_hbm.at[pl.ds(start, TILE)], dst, zs, zr.at[j, same], dev).start()

    z_send(0)

    def image_send(h, side):
        return remote(
            I.at[pl.ds(h * HALF, HALF)],
            I.at[pl.ds((1 + side) * ROWS + h * HALF, HALF)],
            xs, xr.at[side, h], right if side == 0 else left,
        )

    ring = {(h, s): image_send(h, s) for h in range(2) for s in range(2)}
    ring[0, 0].start()
    ring[1, 1].start()

    for cp in local[1:]:
        cp.wait()
    scale = scale_ref[0]
    bias = bias_ref[0]
    ea = -scale * LOG2E
    eb = -bias * LOG2E

    def spread(row):
        return jnp.broadcast_to(row.astype(F32), (TILE, TILE)).T

    for side in range(2):
        for core in range(2):
            def prep(j, carry, side=side, core=core):
                r = (text_blk[side][core] * GROUPS + tp) * TILES + j
                block = 2 * j + side
                rowb[block, pl.ds(core * TILE, TILE), :] = spread(bucket_v[pl.ds(r, 1), :])
                lanes = lax.broadcasted_iota(jnp.int32, blocks_v.shape[1:], 1)
                for l in range(TILES):
                    n = sum(jnp.where(blocks_v[m] == l, 1.0, 0.0) for m in range(SLOTS))
                    n = jnp.sum(jnp.where(lanes == r, n, 0.0), axis=1, keepdims=True)
                    cnt[2 * block + core, l] = jnp.broadcast_to(n * scale, (blocks_v.shape[1], TILE))
                return carry

            lax.fori_loop(0, TILES, prep, 0)

    z_send(1)

    for cp in own_text:
        cp.wait()
    along_y, to_core = [], []
    for j in range(TILES):
        rows = pl.ds(j * TILE, TILE)
        along_y.append([
            remote(pas.at[:, rows], R.at[0, yl, :, rows], ys.at[j], yr.at[j, 0], pair_y),
            remote(pas.at[:, rows], R.at[1, yl, :, rows], ys.at[j], yr.at[j, 1], other_y),
            remote(R.at[0, yl, :, rows], R.at[1, yl, :, rows], ys.at[j], yr.at[j, 2], far_y),
        ])
        to_core.append([
            remote(T.at[2 * j + side, pl.ds(0, TILE)], T.at[2 * j + side, pl.ds(TILE, TILE)], cs, cr.at[j, side], core_dev)
            for side in range(2)
        ])

    def z_ready(j):
        rows = pl.ds(j * TILE, TILE)
        drain(pas.at[pl.ds(0, 3), rows], zr.at[j, 0])
        drain(R.at[0, 0, pl.ds(0, 3), rows], zr.at[j, 1])

    def pass_on(j):
        for cp in along_y[j]:
            cp.start()

    def text_tile(j, side):
        rows = pl.ds(j * TILE, TILE)
        if side == 0:
            along_y[j][0].wait_recv()
        else:
            along_y[j][1].wait_recv()
            along_y[j][2].wait_recv()
        sq = jnp.zeros((TILE, EB), F32)
        for d in range(2):
            for g in range(4):
                v = R[side, d, g, rows, :].astype(F32)
                sq = sq + v * v
        r = lax.rsqrt(jnp.sum(sq, axis=-1, keepdims=True) + 1e-6)
        trs[side, rows, :] = r
        for d in range(2):
            for g in range(4):
                at = (2 * g + d) * EB
                T[2 * j + side, 0:TILE, at : at + EB] = (R[side, d, g, rows, :].astype(F32) * r).astype(BF16)
        to_core[j][side].start()

    def text_ready(j):
        for cp in to_core[j]:
            cp.wait_recv()

    z_ready(0)
    pass_on(0)
    z_send(2)
    z_ready(1)
    ring[1, 0].start()
    ring[0, 1].start()
    drain(pas, ys.at[0])
    pass_on(1)
    on_right = remote(
        I.at[pl.ds(ROWS, HALF)], I.at[pl.ds(3 * ROWS, HALF)], xfs, xfr.at[0], right
    )
    on_left = remote(
        I.at[pl.ds(2 * ROWS + HALF, HALF)], I.at[pl.ds(3 * ROWS + HALF, HALF)],
        xfs, xfr.at[1], left,
    )

    def weights(lo, hi, k0, nk):
        cols = pl.ds(k0 * ROWS, nk * ROWS)

        def body(b, carry):
            s = lax.dot_general(T[b], I[cols, :], NT, preferred_element_type=F32)
            d = 1.0 + jnp.exp2(s * ea + eb)
            for h in range(2):
                rb = rowb[b, pl.ds(h * TILE, TILE), :]
                for k in range(nk):
                    shard = image_blk[k0 + k]
                    for l in range(TILES):
                        tile = (shard * GROUPS + tp) * TILES + l
                        cb = bucket_v[pl.ds(tile, 1), :].astype(F32)
                        co = cnt[2 * b + h, l, pl.ds(shard, 1), :]
                        at = (k * TILES + l) * TILE
                        dd = d[h * TILE : (h + 1) * TILE, at : at + TILE]
                        w = jnp.where(rb == cb, co, 0.0) / dd
                        W[b, pl.ds(h * TILE, TILE), pl.ds(k0 * ROWS + at, TILE)] = w.astype(BF16)
            return carry

        lax.fori_loop(lo, hi, body, 0)

    def own_pairs():
        def body(j, carry):
            at = pl.multiple_of(j * TILE, TILE)
            s = lax.dot_general(
                T[2 * j, 0:TILE, :], I[pl.ds(at, TILE), :], NT, preferred_element_type=F32
            )
            e = jnp.exp2(s * ea + eb)
            tile = (blk * GROUPS + tp) * TILES + j
            rb = rowb[2 * j, 0:TILE, :]
            cb = bucket_v[pl.ds(tile, 1), :].astype(F32)
            co = cnt[4 * j, j, pl.ds(blk, 1), :]
            pos = spread(positive_v[pl.ds(tile, 1), :] - tile * TILE)
            matched = pos == lax.broadcasted_iota(jnp.int32, (TILE, TILE), 1).astype(F32)
            num = jnp.where(matched, -co * e, jnp.where(rb == cb, co, 0.0))
            W[2 * j, 0:TILE, pl.ds(at, TILE)] = (num / (1.0 + e)).astype(BF16)
            return carry

        lax.fori_loop(0, TILES, body, 0)

    def image_sums(k, lo, hi):
        out = None
        for b in range(lo, hi):
            u = lax.dot_general(
                W[b, :, pl.ds(k * ROWS, ROWS)], T[b], TN, preferred_element_type=F32
            )
            out = u if out is None else out + u
        return out

    text_tile(0, 0)
    text_tile(0, 1)
    z_ready(2)
    text_ready(0)
    weights(0, 2, 0, 1)
    drain(pas, ys.at[1])
    pass_on(2)
    ring[0, 0].wait_recv()
    on_right.start()
    ring[1, 1].wait_recv()
    on_left.start()
    text_tile(1, 0)
    text_tile(1, 1)
    text_ready(1)
    ring[1, 0].wait_recv()
    ring[0, 1].wait_recv()
    weights(0, 4, 1, 2)
    pacc[0] = image_sums(2, 0, 4)
    pacc[1] = image_sums(1, 0, 4)
    text_tile(2, 0)
    text_tile(2, 1)
    weights(2, 4, 0, 1)
    text_ready(2)
    weights(4, 6, 1, 2)
    first = pl.ds(0, HALF)
    second = pl.ds(HALF, HALF)
    send_x[1] = (pacc[0] + image_sums(2, 4, 6)).astype(BF16)
    near_right = remote(send_x.at[1, second], got_l.at[second], x2s, x2r.at[0], right)
    near_right.start()
    send_x[0] = (pacc[1] + image_sums(1, 4, 6)).astype(BF16)
    near_left = remote(send_x.at[0, first], got_r.at[first], x2s, x2r.at[1], left)
    near_left.start()

    weights(4, 6, 0, 1)
    own_pairs()
    on_right.wait_recv()
    on_left.wait_recv()
    weights(0, 6, 3, 1)
    partial = [
        remote(send_t.at[b], got_c.at[b], ps, pr.at[b], core_dev) for b in range(2 * TILES)
    ]

    def text_sums(b):
        u = lax.dot_general(W[b], I[...], NN, preferred_element_type=F32)
        tacc[b] = u[0:TILE]
        send_t[b] = u[TILE:].astype(BF16)
        partial[b].start()

    back = []
    for j in range(TILES):
        rows = pl.ds(j * TILE, TILE)
        back.append([
            remote(gsend.at[0, 1 - yl, :, rows], got_pair.at[:, rows], gs, gr.at[j, 0], pair_y),
            remote(gsend.at[1, 1 - yl, :, rows], got_other.at[:, rows], gs, gr.at[j, 1], other_y),
            remote(gsend.at[1, yl, :, rows], got_far.at[:, rows], gs, gr.at[j, 2], far_y),
        ])

    def project(j, side):
        b = 2 * j + side
        rows = pl.ds(j * TILE, TILE)
        partial[b].wait_recv()
        r = trs[side, rows, :]
        up = tacc[b] + got_c[b].astype(F32)
        dot = jnp.zeros((TILE, EB), F32)
        for d in range(2):
            for g in range(4):
                at = (2 * g + d) * EB
                dot = dot + R[side, d, g, rows, :].astype(F32) * r * up[:, at : at + EB]
        total = jnp.sum(dot, axis=-1, keepdims=True)
        for d in range(2):
            for g in range(4):
                at = (2 * g + d) * EB
                u = R[side, d, g, rows, :].astype(F32) * r
                out = r * (up[:, at : at + EB] - u * total)
                gsend[side, d, g, rows, :] = out.astype(BF16)
                if side == 0:
                    keep[d, g, rows, :] = out
        if side == 0:
            back[j][0].start()
        else:
            back[j][1].start()
            back[j][2].start()

    def feature_rows(j):
        rows = pl.ds(j * TILE, TILE)
        for cp in back[j]:
            cp.wait_recv()
        for g in range(4):
            gout[0, g, rows, :] = (
                got_pair[g, rows, :].astype(F32) + got_other[g, rows, :].astype(F32)
            ).astype(BF16)
            gout[1, g, rows, :] = (keep[yl, g, rows, :] + got_far[g, rows, :].astype(F32)).astype(BF16)
        for same in range(2):
            d = 1 - yl if same == 0 else yl
            start = pl.multiple_of((z * 2 + d) * ROWS + j * TILE, TILE)
            for k, dev in z_devs:
                remote(gout.at[same, (z + k) % 4, rows], tgrad_out.at[pl.ds(start, TILE)], o_s, o_r, dev).start()

    PART = HALF // PARTS
    far, summed = {}, {}
    for n in range(PARTS):
        for side, (relay, got, dev) in enumerate(((relay_l, got_l, right), (relay_r, got_r, left))):
            rows = pl.ds(side * HALF + n * PART, PART)
            far[n, side] = remote(
                send_x.at[2, rows], relay.at[pl.ds(n * PART, PART)], x2s, x2r.at[2 + 2 * n + side], dev
            )
            summed[n, side] = remote(
                send_x.at[1 - side, rows], got.at[rows], x2s, x2r.at[2 + 2 * (PARTS + n) + side], dev
            )

    def send_far():
        send_x[2] = image_sums(3, 0, 6).astype(BF16)
        for cp in far.values():
            cp.start()

    def combine(n):
        for side, relay in enumerate((relay_l, relay_r)):
            rows = pl.ds(side * HALF + n * PART, PART)
            far[n, side].wait_recv()
            send_x[1 - side, rows, :] = (
                send_x[1 - side, rows, :].astype(F32) + relay[pl.ds(n * PART, PART), :].astype(F32)
            ).astype(BF16)
            summed[n, side].start()

    text_sums(1)
    text_sums(0)
    project(0, 1)
    text_sums(3)
    project(0, 0)
    send_far()
    text_sums(2)
    project(1, 1)
    text_sums(5)
    project(1, 0)
    text_sums(4)
    project(2, 1)
    iacc[...] = image_sums(0, 0, 6)
    project(2, 0)
    combine(0)
    feature_rows(0)
    combine(1)
    combine(2)
    feature_rows(1)
    feature_rows(2)
    own_out = [
        pltpu.make_async_copy(
            gout.at[same, z], tgrad_out.at[own_rows(1 - yl if same == 0 else yl)], loc_sem.at[8 + same]
        )
        for same in range(2)
    ]
    for cp in own_out:
        cp.start()

    near_right.wait_recv()
    near_left.wait_recv()
    for cp in summed.values():
        cp.wait_recv()
    v = iraw[...].astype(F32) * irs[...]
    up = iacc[...] + got_l[...].astype(F32) + got_r[...].astype(F32)
    d = jnp.sum(v * up, axis=-1, keepdims=True)
    igrad_out[...] = (irs[...] * (up - v * d)).astype(BF16)

    drain(text_hbm.at[pl.ds(0, 6 * ROWS)], zs)
    drain(pas, ys.at[2])
    drain(R.at[:, :, pl.ds(0, 3)], gs)
    drain(I.at[pl.ds(0, 2 * ROWS)], cs)
    drain(I.at[pl.ds(0, 2 * ROWS)], ps)
    drain(I.at[pl.ds(0, ROWS)], xfs)
    drain(I.at[pl.ds(0, 2 * ROWS)], xs)
    drain(I.at[pl.ds(0, 3 * ROWS)], x2s)
    drain(text_hbm.at[pl.ds(0, 6 * ROWS)], o_s)
    drain(tgrad_out.at[pl.ds(0, 6 * ROWS)], o_r)
    for cp in own_out:
        cp.wait()


def per_device(text_emb, image_emb, logit_scale, logit_bias, bucket, positive, blocks):
    vmem_spec = pl.BlockSpec(memory_space=pltpu.VMEM)
    hbm_spec = pl.BlockSpec(memory_space=pltpu.HBM)
    vm = pltpu.VMEM
    dma = pltpu.SemaphoreType.DMA
    tiles = bucket.shape[0] // TILE
    shapes = (
        pltpu.VMEM(text_emb.shape, BF16),
        pltpu.VMEM(image_emb.shape, BF16),
    )
    return pl.pallas_call(
        kernel,
        out_shape=shapes,
        in_specs=[pl.BlockSpec(memory_space=pltpu.SMEM)] * 2 + [hbm_spec] * 5,
        out_specs=(vmem_spec, vmem_spec),
        scratch_shapes=[
            vm((2, 2, 4, ROWS, EB), BF16), vm((4, ROWS, EB), BF16), vm((ROWS, E), BF16),
            vm((tiles, TILE), jnp.int32), vm((tiles, TILE), jnp.int32), vm(blocks.shape[::-1], jnp.int32),
            vm((6, 256, E), BF16), vm((4 * ROWS, E), BF16), vm((6, 256, 4 * ROWS), BF16),
            vm((6, 256, TILE), F32), vm((12, TILES, 16, TILE), F32),
            vm((2, ROWS, 1), F32), vm((ROWS, 1), F32),
            vm((6, TILE, E), F32), vm((ROWS, E), F32), vm((2, ROWS, E), F32),
            vm((6, TILE, E), BF16), vm((3, ROWS, E), BF16), vm((6, TILE, E), BF16),
            vm((ROWS, E), BF16), vm((ROWS, E), BF16), vm((HALF, E), BF16), vm((HALF, E), BF16),
            vm((2, 4, ROWS, EB), F32), vm((2, 2, 4, ROWS, EB), BF16),
            vm((4, ROWS, EB), BF16), vm((4, ROWS, EB), BF16), vm((4, ROWS, EB), BF16),
            vm((2, 4, ROWS, EB), BF16),
            dma((10,)), dma, dma((3, 2)), dma, dma((2, 2)), dma, dma((2,)),
            dma((3,)), dma((3, 3)), dma, dma((3, 2)), dma, dma((6,)), dma, dma((3, 3)),
            dma, dma((2 + 4 * PARTS,)), dma, dma,
        ],
        compiler_params=pltpu.CompilerParams(
            collective_id=0, has_side_effects=True, vmem_limit_bytes=48 << 20
        ),
        name="pairs",
    )(
        logit_scale, logit_bias,
        *(
            pltpu.with_memory_space_constraint(a, pltpu.HBM)
            for a in (
                text_emb, image_emb,
                bucket.reshape(tiles, TILE), positive.reshape(tiles, TILE), blocks.transpose(2, 1, 0),
            )
        )
    )


def solution(mesh):
    in_specs = (P("blk", "tp"), P(("blk", "tp"), None), P(), P(), P(), P(), P())
    out_specs = (P("blk", "tp"), P(("blk", "tp"), None))
    return jax.shard_map(
        per_device, mesh=mesh, in_specs=in_specs, out_specs=out_specs, check_vma=False
    )
```

```python
import jax
import jax.numpy as jnp
from jax import lax
from jax.experimental import pallas as pl
from jax.experimental.pallas import tpu as pltpu
from jax.sharding import PartitionSpec as P

MESH = pl.DeviceIdType.MESH
F32 = jnp.float32
BF16 = jnp.bfloat16
TILE = 128
TILES = 3
SLOTS = 3
ROWS = TILE * TILES
HALF = ROWS // 2
CHUNKS = 4
PARTS = 3
E = 1024
GROUPS = 8
EB = E // GROUPS
LOG2E = 1.4426950408889634
NT = (((1,), (1,)), ((), ()))
NN = (((1,), (0,)), ((), ()))
TN = (((0,), (0,)), ((), ()))


def kernel(
    scale_ref, bias_ref, text_hbm, image_hbm, bucket_hbm, positive_hbm, blocks_hbm,
    tgrad_out, igrad_out,
    R, pas, iraw, bucket_v, positive_v, blocks_v,
    T, I, W, M, rowb, cnt, trs, irs,
    tacc, iacc, send_t, send_x, got_c, got_l, got_r, relay_l, relay_r,
    keep, gsend, got_far, got_pair, got_other, gout,
    loc_sem, zs, zr, xs, xr, xfs, xfr, y0s, y0r, ys, yr, cs, cr, ps, pr, gs, gr, x2s, x2r, o_s, o_r,
):
    blk = lax.axis_index("blk")
    tp = lax.axis_index("tp")
    yh = blk // 8
    x = (blk // 2) % 4
    c = blk % 2
    z = tp // 2
    yl = tp % 2
    yh_blk = (blk + 8) % 16
    tp_pair = tp + 1 - 2 * yl
    core_dev = (blk + 1 - 2 * c, tp)
    far_y = (yh_blk, tp)
    pair_y = (blk, tp_pair)
    other_y = (yh_blk, tp_pair)
    z_devs = [(k, (blk, ((z + k) % 4) * 2 + yl)) for k in range(1, 4)]
    right = ((yh * 4 + (x + 1) % 4) * 2 + c, tp)
    left = ((yh * 4 + (x + 3) % 4) * 2 + c, tp)
    far_blk = (yh * 4 + (x + 2) % 4) * 2 + c
    image_blk = (blk, left[0], right[0], far_blk)
    text_blk = ((blk, core_dev[0]), (yh_blk, yh_blk + 1 - 2 * c))

    def remote(src, dst, ssem, rsem, dev):
        return pltpu.make_async_remote_copy(
            src_ref=src, dst_ref=dst, send_sem=ssem, recv_sem=rsem,
            device_id=dev, device_id_type=MESH,
        )

    def drain(ref, sem):
        pltpu.make_async_copy(ref, ref, sem).wait()

    local = [
        pltpu.make_async_copy(image_hbm, iraw, loc_sem.at[0]),
        pltpu.make_async_copy(bucket_hbm, bucket_v, loc_sem.at[1]),
        pltpu.make_async_copy(positive_hbm, positive_v, loc_sem.at[2]),
        pltpu.make_async_copy(blocks_hbm, blocks_v, loc_sem.at[3]),
    ]
    def own_rows(d):
        return pl.ds(pl.multiple_of((z * 2 + d) * ROWS, ROWS), ROWS)

    own_text = pltpu.make_async_copy(text_hbm.at[own_rows(yl)], R.at[0, yl, z], loc_sem.at[6])
    for cp in local:
        cp.start()
    own_text.start()

    barrier = pltpu.get_barrier_semaphore()
    peers = [dev for _, dev in z_devs] + [far_y, pair_y, other_y, core_dev, right, left]
    for dev in peers:
        pl.semaphore_signal(barrier, inc=1, device_id=dev, device_id_type=MESH)

    local[0].wait()
    for h in range(2):
        rows = pl.ds(h * HALF, HALF)
        v = iraw[rows, :].astype(F32)
        r = lax.rsqrt(jnp.sum(v * v, axis=-1, keepdims=True) + 1e-6)
        irs[rows, :] = r
        I[rows, :] = (v * r).astype(BF16)

    pl.semaphore_wait(barrier, len(peers))

    def z_send(j):
        rows = pl.ds(j * TILE, TILE)
        for k, dev in z_devs:
            base = ((z + k) % 4) * 2
            for same in range(2):
                d = 1 - yl if same == 0 else yl
                start = pl.multiple_of((base + d) * ROWS + j * TILE, TILE)
                dst = R.at[0, yl, z, rows] if same else pas.at[z, rows]
                remote(text_hbm.at[pl.ds(start, TILE)], dst, zs, zr.at[j, same], dev).start()

    z_send(0)
    held = [
        remote(text_hbm.at[own_rows(1 - yl)], R.at[0, yl, z], y0s, y0r.at[0], pair_y),
        remote(text_hbm.at[own_rows(1 - yl)], R.at[1, yl, z], y0s, y0r.at[1], other_y),
        remote(text_hbm.at[own_rows(yl)], R.at[1, yl, z], y0s, y0r.at[2], far_y),
    ]
    for cp in held:
        cp.start()

    def image_send(h, side):
        return remote(
            I.at[pl.ds(h * HALF, HALF)],
            I.at[pl.ds((1 + side) * ROWS + h * HALF, HALF)],
            xs, xr.at[side, h], right if side == 0 else left,
        )

    ring = {(h, s): image_send(h, s) for h in range(2) for s in range(2)}
    ring[0, 0].start()
    ring[1, 1].start()

    for cp in local[1:]:
        cp.wait()
    scale = scale_ref[0]
    bias = bias_ref[0]
    ea = -scale * LOG2E
    eb = -bias * LOG2E

    def spread(row):
        return jnp.broadcast_to(row.astype(F32), (TILE, TILE)).T

    for side in range(2):
        for core in range(2):
            def prep(j, carry, side=side, core=core):
                r = (text_blk[side][core] * GROUPS + tp) * TILES + j
                block = 2 * j + side
                rowb[block, pl.ds(core * TILE, TILE), :] = spread(bucket_v[pl.ds(r, 1), :])
                lanes = lax.broadcasted_iota(jnp.int32, blocks_v.shape[1:], 1)
                for l in range(TILES):
                    n = sum(jnp.where(blocks_v[m] == l, 1.0, 0.0) for m in range(SLOTS))
                    n = jnp.sum(jnp.where(lanes == r, n, 0.0), axis=1, keepdims=True)
                    cnt[2 * block + core, l] = jnp.broadcast_to(n, (blocks_v.shape[1], TILE))
                return carry

            lax.fori_loop(0, TILES, prep, 0)

    z_send(1)

    def pair_masks(b, carry):
        for k in range(4):
            for l in range(TILES):
                cb = bucket_v[pl.ds((image_blk[k] * GROUPS + tp) * TILES + l, 1), :].astype(F32)
                for h in range(2):
                    rows = pl.ds(pl.multiple_of((2 * b + h) * TILE, TILE), TILE)
                    n = cnt[2 * b + h, l, pl.ds(image_blk[k], 1), :]
                    M[rows, pl.ds(k * ROWS + l * TILE, TILE)] = jnp.where(
                        rowb[b, pl.ds(h * TILE, TILE), :] == cb, n, 0.0
                    ).astype(BF16)
        return carry

    lax.fori_loop(0, 2 * TILES, pair_masks, 0)

    own_text.wait()
    along_y, to_core = [], []
    for j in range(TILES):
        rows = pl.ds(j * TILE, TILE)
        pieces = []
        for k in range(1, 4):
            zk = (z + k) % 4
            pieces += [
                remote(pas.at[zk, rows], R.at[0, yl, zk, rows], ys.at[j], yr.at[j, 0], pair_y),
                remote(pas.at[zk, rows], R.at[1, yl, zk, rows], ys.at[j], yr.at[j, 1], other_y),
                remote(R.at[0, yl, zk, rows], R.at[1, yl, zk, rows], ys.at[j], yr.at[j, 2], far_y),
            ]
        along_y.append(pieces)
        to_core.append([
            remote(T.at[pl.ds((4 * j + 2 * side) * TILE, TILE)], T.at[pl.ds((4 * j + 2 * side + 1) * TILE, TILE)], cs, cr.at[j, side], core_dev)
            for side in range(2)
        ])

    def z_ready(j):
        rows = pl.ds(j * TILE, TILE)
        drain(pas.at[pl.ds(0, 3), rows], zr.at[j, 0])
        drain(R.at[0, 0, pl.ds(0, 3), rows], zr.at[j, 1])

    def pass_on(j):
        for cp in along_y[j]:
            cp.start()

    def text_tile(j, side):
        rows = pl.ds(j * TILE, TILE)
        for kind in (0,) if side == 0 else (1, 2):
            if j == 0:
                held[kind].wait_recv()
            drain(pas.at[pl.ds(0, 3), rows], yr.at[j, kind])
        sq = jnp.zeros((TILE, EB), F32)
        for d in range(2):
            for g in range(4):
                v = R[side, d, g, rows, :].astype(F32)
                sq = sq + v * v
        r = lax.rsqrt(jnp.sum(sq, axis=-1, keepdims=True) + 1e-6)
        trs[side, rows, :] = r
        for d in range(2):
            for g in range(4):
                at = (2 * g + d) * EB
                T[pl.ds((4 * j + 2 * side) * TILE, TILE), at : at + EB] = (R[side, d, g, rows, :].astype(F32) * r).astype(BF16)
        to_core[j][side].start()

    def text_ready(j):
        for cp in to_core[j]:
            cp.wait_recv()

    z_ready(0)
    pass_on(0)
    z_send(2)
    z_ready(1)
    pass_on(1)
    ring[1, 0].start()
    ring[0, 1].start()
    z_ready(2)
    pass_on(2)
    on_right = remote(
        I.at[pl.ds(ROWS, HALF)], I.at[pl.ds(3 * ROWS, HALF)], xfs, xfr.at[0], right
    )
    on_left = remote(
        I.at[pl.ds(2 * ROWS + HALF, HALF)], I.at[pl.ds(3 * ROWS + HALF, HALF)],
        xfs, xfr.at[1], left,
    )

    def weights(lo, hi, k0, nk):
        cols = pl.ds(k0 * ROWS, nk * ROWS)

        for b in range(lo, hi):
            rows = pl.ds(b * 2 * TILE, 2 * TILE)
            s = lax.dot_general(T[rows, :], I[cols, :], NT, preferred_element_type=F32)
            w = pl.reciprocal(1.0 + jnp.exp2(s * ea + eb)).astype(BF16)
            W[rows, cols] = w * M[rows, cols]

    def own_pairs(j):
        at = j * TILE
        s = lax.dot_general(T[4 * at : 4 * at + TILE, :], I[at : at + TILE, :], NT, preferred_element_type=F32)
        e = jnp.exp2(s * ea + eb)
        tile = (blk * GROUPS + tp) * TILES + j
        n = cnt[4 * j, j, pl.ds(blk, 1), :]
        pos = spread(positive_v[pl.ds(tile, 1), :] - tile * TILE)
        matched = pos == lax.broadcasted_iota(jnp.int32, (TILE, TILE), 1).astype(F32)
        num = jnp.where(matched, -n * e, M[4 * at : 4 * at + TILE, at : at + TILE].astype(F32))
        W[4 * at : 4 * at + TILE, at : at + TILE] = (num / (1.0 + e)).astype(BF16)

    def image_sums(k):
        return lax.dot_general(W[:, pl.ds(k * ROWS, ROWS)], T[...], TN, preferred_element_type=F32)

    text_tile(0, 0)
    text_tile(0, 1)
    text_ready(0)
    weights(0, 2, 0, 1)
    own_pairs(0)
    ring[0, 0].wait_recv()
    on_right.start()
    ring[1, 1].wait_recv()
    on_left.start()
    text_tile(1, 0)
    text_tile(1, 1)
    text_ready(1)
    weights(2, 4, 0, 1)
    own_pairs(1)
    text_tile(2, 0)
    text_tile(2, 1)
    text_ready(2)
    weights(4, 6, 0, 1)
    own_pairs(2)
    ring[1, 0].wait_recv()
    ring[0, 1].wait_recv()
    weights(0, 6, 1, 2)
    first = pl.ds(0, HALF)
    second = pl.ds(HALF, HALF)
    send_x[1] = image_sums(2).astype(BF16)
    near_right = remote(send_x.at[1, second], got_l.at[second], x2s, x2r.at[0], right)
    near_right.start()
    send_x[0] = image_sums(1).astype(BF16)
    near_left = remote(send_x.at[0, first], got_r.at[first], x2s, x2r.at[1], left)
    near_left.start()
    on_right.wait_recv()
    on_left.wait_recv()
    weights(0, 6, 3, 1)
    partial = [
        remote(send_t.at[b], got_c.at[b], ps, pr.at[b], core_dev) for b in range(2 * TILES)
    ]

    def text_sums(b):
        u = lax.dot_general(W[pl.ds(b * 2 * TILE, 2 * TILE), :], I[...], NN, preferred_element_type=F32)
        tacc[b] = u[0:TILE]
        send_t[b] = u[TILE:].astype(BF16)
        partial[b].start()

    back = []
    for j in range(TILES):
        rows = pl.ds(j * TILE, TILE)
        back.append([
            remote(gsend.at[0, 1 - yl, :, rows], got_pair.at[:, rows], gs, gr.at[j, 0], pair_y),
            remote(gsend.at[1, 1 - yl, :, rows], got_other.at[:, rows], gs, gr.at[j, 1], other_y),
            remote(gsend.at[1, yl, :, rows], got_far.at[:, rows], gs, gr.at[j, 2], far_y),
        ])

    def project(j, side):
        b = 2 * j + side
        rows = pl.ds(j * TILE, TILE)
        partial[b].wait_recv()
        r = trs[side, rows, :]
        rs = r * scale
        up = tacc[b] + got_c[b].astype(F32)
        dot = jnp.zeros((TILE, EB), F32)
        for d in range(2):
            for g in range(4):
                at = (2 * g + d) * EB
                dot = dot + R[side, d, g, rows, :].astype(F32) * r * up[:, at : at + EB]
        total = jnp.sum(dot, axis=-1, keepdims=True)
        for d in range(2):
            for g in range(4):
                at = (2 * g + d) * EB
                u = R[side, d, g, rows, :].astype(F32) * r
                out = rs * (up[:, at : at + EB] - u * total)
                gsend[side, d, g, rows, :] = out.astype(BF16)
                if side == 0:
                    keep[d, g, rows, :] = out
        if side == 0:
            back[j][0].start()
        else:
            back[j][1].start()
            back[j][2].start()

    def feature_rows(j):
        rows = pl.ds(j * TILE, TILE)
        for cp in back[j]:
            cp.wait_recv()
        for g in range(4):
            gout[0, g, rows, :] = (
                got_pair[g, rows, :].astype(F32) + got_other[g, rows, :].astype(F32)
            ).astype(BF16)
            gout[1, g, rows, :] = (keep[yl, g, rows, :] + got_far[g, rows, :].astype(F32)).astype(BF16)
        for same in range(2):
            d = 1 - yl if same == 0 else yl
            start = pl.multiple_of((z * 2 + d) * ROWS + j * TILE, TILE)
            for k, dev in z_devs:
                remote(gout.at[same, (z + k) % 4, rows], tgrad_out.at[pl.ds(start, TILE)], o_s, o_r, dev).start()

    PART = HALF // PARTS
    far, summed = {}, {}
    for n in range(PARTS):
        for side, (relay, got, dev) in enumerate(((relay_l, got_l, right), (relay_r, got_r, left))):
            rows = pl.ds(side * HALF + n * PART, PART)
            far[n, side] = remote(
                send_x.at[2, rows], relay.at[pl.ds(n * PART, PART)], x2s, x2r.at[2 + 2 * n + side], dev
            )
            summed[n, side] = remote(
                send_x.at[1 - side, rows], got.at[rows], x2s, x2r.at[2 + 2 * (PARTS + n) + side], dev
            )

    def send_far():
        send_x[2] = image_sums(3).astype(BF16)
        for cp in far.values():
            cp.start()

    def combine(n):
        for side, relay in enumerate((relay_l, relay_r)):
            rows = pl.ds(side * HALF + n * PART, PART)
            far[n, side].wait_recv()
            send_x[1 - side, rows, :] = (
                send_x[1 - side, rows, :].astype(F32) + relay[pl.ds(n * PART, PART), :].astype(F32)
            ).astype(BF16)
            summed[n, side].start()

    text_sums(1)
    text_sums(0)
    project(0, 1)
    text_sums(3)
    project(0, 0)
    send_far()
    text_sums(2)
    project(1, 1)
    text_sums(5)
    project(1, 0)
    text_sums(4)
    project(2, 1)
    iacc[...] = image_sums(0)
    project(2, 0)
    combine(0)
    feature_rows(0)
    combine(1)
    combine(2)
    feature_rows(1)
    feature_rows(2)
    own_out = [
        pltpu.make_async_copy(
            gout.at[same, z], tgrad_out.at[own_rows(1 - yl if same == 0 else yl)], loc_sem.at[8 + same]
        )
        for same in range(2)
    ]
    for cp in own_out:
        cp.start()

    near_right.wait_recv()
    near_left.wait_recv()
    for cp in summed.values():
        cp.wait_recv()
    v = iraw[...].astype(F32) * irs[...]
    up = iacc[...] + got_l[...].astype(F32) + got_r[...].astype(F32)
    d = jnp.sum(v * up, axis=-1, keepdims=True)
    igrad_out[...] = (irs[...] * scale * (up - v * d)).astype(BF16)

    drain(text_hbm.at[pl.ds(0, 6 * ROWS)], zs)
    for j in range(TILES):
        drain(R.at[0, 0, pl.ds(0, 3)], ys.at[j])
    drain(R.at[0, 0, pl.ds(0, 3)], y0s)
    drain(R.at[:, :, pl.ds(0, 3)], gs)
    drain(I.at[pl.ds(0, 2 * ROWS)], cs)
    drain(I.at[pl.ds(0, 2 * ROWS)], ps)
    drain(I.at[pl.ds(0, ROWS)], xfs)
    drain(I.at[pl.ds(0, 2 * ROWS)], xs)
    drain(I.at[pl.ds(0, 3 * ROWS)], x2s)
    drain(text_hbm.at[pl.ds(0, 6 * ROWS)], o_s)
    drain(tgrad_out.at[pl.ds(0, 6 * ROWS)], o_r)
    for cp in own_out:
        cp.wait()


def write_out(a_ref, b_ref, a_out, b_out, sem):
    copies = []
    for src, dst in ((a_ref, a_out), (b_ref, b_out)):
        step = src.shape[0] // CHUNKS
        for n in range(CHUNKS):
            rows = pl.ds(n * step, step)
            copies.append(pltpu.make_async_copy(src.at[rows], dst.at[rows], sem.at[len(copies)]))
    for cp in copies:
        cp.start()
    for cp in copies:
        cp.wait()


def per_device(text_emb, image_emb, logit_scale, logit_bias, bucket, positive, blocks):
    vmem_spec = pl.BlockSpec(memory_space=pltpu.VMEM)
    hbm_spec = pl.BlockSpec(memory_space=pltpu.HBM)
    vm = pltpu.VMEM
    dma = pltpu.SemaphoreType.DMA
    tiles = bucket.shape[0] // TILE
    shapes = (
        pltpu.VMEM(text_emb.shape, BF16),
        pltpu.VMEM(image_emb.shape, BF16),
    )
    grads = pl.pallas_call(
        kernel,
        out_shape=shapes,
        in_specs=[pl.BlockSpec(memory_space=pltpu.SMEM)] * 2 + [hbm_spec] * 5,
        out_specs=(vmem_spec, vmem_spec),
        scratch_shapes=[
            vm((2, 2, 4, ROWS, EB), BF16), vm((4, ROWS, EB), BF16), vm((ROWS, E), BF16),
            vm((tiles, TILE), jnp.int32), vm((tiles, TILE), jnp.int32), vm(blocks.shape[::-1], jnp.int32),
            vm((4 * ROWS, E), BF16), vm((4 * ROWS, E), BF16), vm((4 * ROWS, 4 * ROWS), BF16), vm((4 * ROWS, 4 * ROWS), BF16),
            vm((6, 256, TILE), F32), vm((12, TILES, 16, TILE), F32),
            vm((2, ROWS, 1), F32), vm((ROWS, 1), F32),
            vm((6, TILE, E), F32), vm((ROWS, E), F32),
            vm((6, TILE, E), BF16), vm((3, ROWS, E), BF16), vm((6, TILE, E), BF16),
            vm((ROWS, E), BF16), vm((ROWS, E), BF16), vm((HALF, E), BF16), vm((HALF, E), BF16),
            vm((2, 4, ROWS, EB), F32), vm((2, 2, 4, ROWS, EB), BF16),
            vm((4, ROWS, EB), BF16), vm((4, ROWS, EB), BF16), vm((4, ROWS, EB), BF16),
            vm((2, 4, ROWS, EB), BF16),
            dma((10,)), dma, dma((3, 2)), dma, dma((2, 2)), dma, dma((2,)),
            dma, dma((3,)), dma((3,)), dma((3, 3)), dma, dma((3, 2)), dma, dma((6,)), dma, dma((3, 3)),
            dma, dma((2 + 4 * PARTS,)), dma, dma,
        ],
        compiler_params=pltpu.CompilerParams(
            collective_id=0, has_side_effects=True, vmem_limit_bytes=48 << 20
        ),
        name="pairs",
    )(
        logit_scale, logit_bias,
        *(
            pltpu.with_memory_space_constraint(a, pltpu.HBM)
            for a in (
                text_emb, image_emb,
                bucket.reshape(tiles, TILE), positive.reshape(tiles, TILE), blocks.transpose(2, 1, 0),
            )
        )
    )
    return pl.pallas_call(
        write_out,
        out_shape=(
            jax.ShapeDtypeStruct(text_emb.shape, BF16),
            jax.ShapeDtypeStruct(image_emb.shape, BF16),
        ),
        in_specs=[vmem_spec, vmem_spec],
        out_specs=(hbm_spec, hbm_spec),
        scratch_shapes=[dma((2 * CHUNKS,))],
        name="write_out",
    )(*(pltpu.with_memory_space_constraint(a, pltpu.VMEM) for a in grads))


def solution(mesh):
    in_specs = (P("blk", "tp"), P(("blk", "tp"), None), P(), P(), P(), P(), P())
    out_specs = (P("blk", "tp"), P(("blk", "tp"), None))
    return jax.shard_map(
        per_device, mesh=mesh, in_specs=in_specs, out_specs=out_specs, check_vma=False
    )
```

```python
import jax
import jax.numpy as jnp
from jax import lax
from jax.experimental import pallas as pl
from jax.experimental.pallas import tpu as pltpu
from jax.sharding import PartitionSpec as P

MESH = pl.DeviceIdType.MESH
F32 = jnp.float32
BF16 = jnp.bfloat16
TILE = 128
TILES = 3
SLOTS = 3
ROWS = TILE * TILES
HALF = ROWS // 2
CHUNKS = 4
PARTS = 3
E = 1024
GROUPS = 8
EB = E // GROUPS
LOG2E = 1.4426950408889634
NT = (((1,), (1,)), ((), ()))
NN = (((1,), (0,)), ((), ()))
TN = (((0,), (0,)), ((), ()))


def kernel(
    scale_ref, bias_ref, text_hbm, image_hbm, bucket_hbm, positive_hbm, blocks_hbm,
    tgrad_out, igrad_out,
    R, pas, iraw, bucket_v, positive_v, blocks_v,
    T, I, W, M, rowb, cnt, trs, irs,
    tacc, iacc, send_t, send_x, got_c, got_l, got_r, relay_l, relay_r,
    keep, gsend, got_far, got_pair, got_other, gout,
    loc_sem, zs, zr, xs, xr, xfs, xfr, y0s, y0r, ys, yr, cs, cr, ps, pr, gs, gr, x2s, x2r, o_s, o_r,
):
    blk = lax.axis_index("blk")
    tp = lax.axis_index("tp")
    yh = blk // 8
    x = (blk // 2) % 4
    c = blk % 2
    z = tp // 2
    yl = tp % 2
    yh_blk = (blk + 8) % 16
    tp_pair = tp + 1 - 2 * yl
    core_dev = (blk + 1 - 2 * c, tp)
    far_y = (yh_blk, tp)
    pair_y = (blk, tp_pair)
    other_y = (yh_blk, tp_pair)
    z_devs = [(k, (blk, ((z + k) % 4) * 2 + yl)) for k in range(1, 4)]
    right = ((yh * 4 + (x + 1) % 4) * 2 + c, tp)
    left = ((yh * 4 + (x + 3) % 4) * 2 + c, tp)
    far_blk = (yh * 4 + (x + 2) % 4) * 2 + c
    image_blk = (blk, left[0], right[0], far_blk)
    text_blk = ((blk, core_dev[0]), (yh_blk, yh_blk + 1 - 2 * c))

    def remote(src, dst, ssem, rsem, dev):
        return pltpu.make_async_remote_copy(
            src_ref=src, dst_ref=dst, send_sem=ssem, recv_sem=rsem,
            device_id=dev, device_id_type=MESH,
        )

    def drain(ref, sem):
        pltpu.make_async_copy(ref, ref, sem).wait()

    local = [
        pltpu.make_async_copy(image_hbm, iraw, loc_sem.at[0]),
        pltpu.make_async_copy(bucket_hbm, bucket_v, loc_sem.at[1]),
        pltpu.make_async_copy(positive_hbm, positive_v, loc_sem.at[2]),
        pltpu.make_async_copy(blocks_hbm, blocks_v, loc_sem.at[3]),
    ]
    def own_rows(d):
        return pl.ds(pl.multiple_of((z * 2 + d) * ROWS, ROWS), ROWS)

    own_text = pltpu.make_async_copy(text_hbm.at[own_rows(yl)], R.at[0, yl, z], loc_sem.at[6])
    for cp in local:
        cp.start()
    own_text.start()

    barrier = pltpu.get_barrier_semaphore()
    peers = [dev for _, dev in z_devs] + [far_y, pair_y, other_y, core_dev, right, left]
    for dev in peers:
        pl.semaphore_signal(barrier, inc=1, device_id=dev, device_id_type=MESH)

    local[0].wait()
    for h in range(2):
        rows = pl.ds(h * HALF, HALF)
        v = iraw[rows, :].astype(F32)
        r = lax.rsqrt(jnp.sum(v * v, axis=-1, keepdims=True) + 1e-6)
        irs[rows, :] = r
        I[rows, :] = (v * r).astype(BF16)

    pl.semaphore_wait(barrier, len(peers))

    def z_send(j):
        rows = pl.ds(j * TILE, TILE)
        for k, dev in z_devs:
            base = ((z + k) % 4) * 2
            for same in range(2):
                d = 1 - yl if same == 0 else yl
                start = pl.multiple_of((base + d) * ROWS + j * TILE, TILE)
                dst = R.at[0, yl, z, rows] if same else pas.at[z, rows]
                remote(text_hbm.at[pl.ds(start, TILE)], dst, zs, zr.at[j, same], dev).start()

    z_send(0)
    held = [
        remote(text_hbm.at[own_rows(1 - yl)], R.at[0, yl, z], y0s, y0r.at[0], pair_y),
        remote(text_hbm.at[own_rows(1 - yl)], R.at[1, yl, z], y0s, y0r.at[1], other_y),
        remote(text_hbm.at[own_rows(yl)], R.at[1, yl, z], y0s, y0r.at[2], far_y),
    ]
    for cp in held:
        cp.start()

    def image_send(h, side):
        return remote(
            I.at[pl.ds(h * HALF, HALF)],
            I.at[pl.ds((1 + side) * ROWS + h * HALF, HALF)],
            xs, xr.at[side, h], right if side == 0 else left,
        )

    ring = {(h, s): image_send(h, s) for h in range(2) for s in range(2)}
    ring[0, 0].start()
    ring[1, 1].start()

    for cp in local[1:]:
        cp.wait()
    scale = scale_ref[0]
    bias = bias_ref[0]
    ea = -scale * LOG2E
    eb = -bias * LOG2E

    def spread(row):
        return jnp.broadcast_to(row.astype(F32), (TILE, TILE)).T

    for side in range(2):
        for core in range(2):
            def prep(j, carry, side=side, core=core):
                r = (text_blk[side][core] * GROUPS + tp) * TILES + j
                block = 2 * j + side
                rowb[block, pl.ds(core * TILE, TILE), :] = spread(bucket_v[pl.ds(r, 1), :])
                lanes = lax.broadcasted_iota(jnp.int32, blocks_v.shape[1:], 1)
                for l in range(TILES):
                    n = sum(jnp.where(blocks_v[m] == l, 1.0, 0.0) for m in range(SLOTS))
                    n = jnp.sum(jnp.where(lanes == r, n, 0.0), axis=1, keepdims=True)
                    cnt[2 * block + core, l] = jnp.broadcast_to(n, (blocks_v.shape[1], TILE))
                return carry

            lax.fori_loop(0, TILES, prep, 0)

    z_send(1)

    def pair_masks(b, carry):
        for k in range(4):
            for l in range(TILES):
                cb = bucket_v[pl.ds((image_blk[k] * GROUPS + tp) * TILES + l, 1), :].astype(F32)
                for h in range(2):
                    rows = pl.ds(pl.multiple_of((2 * b + h) * TILE, TILE), TILE)
                    n = cnt[2 * b + h, l, pl.ds(image_blk[k], 1), :]
                    M[rows, pl.ds(k * ROWS + l * TILE, TILE)] = jnp.where(
                        rowb[b, pl.ds(h * TILE, TILE), :] == cb, n, 0.0
                    ).astype(BF16)
        return carry

    lax.fori_loop(0, 2 * TILES, pair_masks, 0)

    own_text.wait()
    along_y, to_core = [], []
    for j in range(TILES):
        rows = pl.ds(j * TILE, TILE)
        pieces = []
        for k in range(1, 4):
            zk = (z + k) % 4
            pieces += [
                remote(pas.at[zk, rows], R.at[0, yl, zk, rows], ys.at[j], yr.at[j, 0], pair_y),
                remote(pas.at[zk, rows], R.at[1, yl, zk, rows], ys.at[j], yr.at[j, 1], other_y),
                remote(R.at[0, yl, zk, rows], R.at[1, yl, zk, rows], ys.at[j], yr.at[j, 2], far_y),
            ]
        along_y.append(pieces)
        to_core.append([
            remote(T.at[pl.ds((4 * j + 2 * side) * TILE, TILE)], T.at[pl.ds((4 * j + 2 * side + 1) * TILE, TILE)], cs, cr.at[j, side], core_dev)
            for side in range(2)
        ])

    def z_ready(j):
        rows = pl.ds(j * TILE, TILE)
        drain(pas.at[pl.ds(0, 3), rows], zr.at[j, 0])
        drain(R.at[0, 0, pl.ds(0, 3), rows], zr.at[j, 1])

    def pass_on(j):
        for cp in along_y[j]:
            cp.start()

    def text_tile(j, side):
        rows = pl.ds(j * TILE, TILE)
        for kind in (0,) if side == 0 else (1, 2):
            if j == 0:
                held[kind].wait_recv()
            drain(pas.at[pl.ds(0, 3), rows], yr.at[j, kind])
        sq = jnp.zeros((TILE, EB), F32)
        for d in range(2):
            for g in range(4):
                v = R[side, d, g, rows, :].astype(F32)
                sq = sq + v * v
        r = lax.rsqrt(jnp.sum(sq, axis=-1, keepdims=True) + 1e-6)
        trs[side, rows, :] = r
        for d in range(2):
            for g in range(4):
                at = (2 * g + d) * EB
                T[pl.ds((4 * j + 2 * side) * TILE, TILE), at : at + EB] = (R[side, d, g, rows, :].astype(F32) * r).astype(BF16)
        to_core[j][side].start()

    def text_ready(j):
        for cp in to_core[j]:
            cp.wait_recv()

    z_ready(0)
    pass_on(0)
    z_send(2)
    z_ready(1)
    pass_on(1)
    ring[1, 0].start()
    ring[0, 1].start()
    z_ready(2)
    pass_on(2)
    on_right = remote(
        I.at[pl.ds(ROWS, HALF)], I.at[pl.ds(3 * ROWS, HALF)], xfs, xfr.at[0], right
    )
    on_left = remote(
        I.at[pl.ds(2 * ROWS + HALF, HALF)], I.at[pl.ds(3 * ROWS + HALF, HALF)],
        xfs, xfr.at[1], left,
    )

    def weights(blocks, k0, nk):
        cols = pl.ds(k0 * ROWS, nk * ROWS)

        for b in blocks:
            rows = pl.ds(b * 2 * TILE, 2 * TILE)
            s = lax.dot_general(T[rows, :], I[cols, :], NT, preferred_element_type=F32)
            w = pl.reciprocal(1.0 + jnp.exp2(s * ea + eb)).astype(BF16)
            W[rows, cols] = w * M[rows, cols]

    def own_pairs(j):
        at = j * TILE
        s = lax.dot_general(T[4 * at : 4 * at + TILE, :], I[at : at + TILE, :], NT, preferred_element_type=F32)
        e = jnp.exp2(s * ea + eb)
        tile = (blk * GROUPS + tp) * TILES + j
        n = cnt[4 * j, j, pl.ds(blk, 1), :]
        pos = spread(positive_v[pl.ds(tile, 1), :] - tile * TILE)
        matched = pos == lax.broadcasted_iota(jnp.int32, (TILE, TILE), 1).astype(F32)
        num = jnp.where(matched, -n * e, M[4 * at : 4 * at + TILE, at : at + TILE].astype(F32))
        W[4 * at : 4 * at + TILE, at : at + TILE] = (num / (1.0 + e)).astype(BF16)

    def image_sums(k):
        return lax.dot_general(W[:, pl.ds(k * ROWS, ROWS)], T[...], TN, preferred_element_type=F32)

    text_tile(0, 0)
    text_tile(0, 1)
    text_ready(0)
    weights((0, 1), 0, 1)
    own_pairs(0)
    ring[0, 0].wait_recv()
    on_right.start()
    ring[1, 1].wait_recv()
    on_left.start()
    text_tile(1, 0)
    text_tile(1, 1)
    text_ready(1)
    text_tile(2, 0)
    text_tile(2, 1)
    ring[1, 0].wait_recv()
    ring[0, 1].wait_recv()
    weights(range(4), 1, 2)
    text_ready(2)
    weights((4, 5), 2, 1)
    first = pl.ds(0, HALF)
    second = pl.ds(HALF, HALF)
    send_x[1] = image_sums(2).astype(BF16)
    near_right = remote(send_x.at[1, second], got_l.at[second], x2s, x2r.at[0], right)
    near_right.start()
    weights((4, 5), 1, 1)
    send_x[0] = image_sums(1).astype(BF16)
    near_left = remote(send_x.at[0, first], got_r.at[first], x2s, x2r.at[1], left)
    near_left.start()
    on_right.wait_recv()
    on_left.wait_recv()
    partial = [
        remote(send_t.at[b], got_c.at[b], ps, pr.at[b], core_dev) for b in range(2 * TILES)
    ]

    def text_sums(b):
        u = lax.dot_general(W[pl.ds(b * 2 * TILE, 2 * TILE), :], I[...], NN, preferred_element_type=F32)
        tacc[b] = u[0:TILE]
        send_t[b] = u[TILE:].astype(BF16)
        partial[b].start()

    back = []
    for j in range(TILES):
        rows = pl.ds(j * TILE, TILE)
        back.append([
            remote(gsend.at[0, 1 - yl, :, rows], got_pair.at[:, rows], gs, gr.at[j, 0], pair_y),
            remote(gsend.at[1, 1 - yl, :, rows], got_other.at[:, rows], gs, gr.at[j, 1], other_y),
            remote(gsend.at[1, yl, :, rows], got_far.at[:, rows], gs, gr.at[j, 2], far_y),
        ])

    def project(j, side):
        b = 2 * j + side
        rows = pl.ds(j * TILE, TILE)
        partial[b].wait_recv()
        r = trs[side, rows, :]
        rs = r * scale
        up = tacc[b] + got_c[b].astype(F32)
        dot = jnp.zeros((TILE, EB), F32)
        for d in range(2):
            for g in range(4):
                at = (2 * g + d) * EB
                dot = dot + R[side, d, g, rows, :].astype(F32) * r * up[:, at : at + EB]
        total = jnp.sum(dot, axis=-1, keepdims=True)
        for d in range(2):
            for g in range(4):
                at = (2 * g + d) * EB
                u = R[side, d, g, rows, :].astype(F32) * r
                out = rs * (up[:, at : at + EB] - u * total)
                gsend[side, d, g, rows, :] = out.astype(BF16)
                if side == 0:
                    keep[d, g, rows, :] = out
        if side == 0:
            back[j][0].start()
        else:
            back[j][1].start()
            back[j][2].start()

    def feature_rows(j, same):
        rows = pl.ds(j * TILE, TILE)
        for cp in back[j][2:] if same else back[j][:2]:
            cp.wait_recv()
        for g in range(4):
            if same:
                out = keep[yl, g, rows, :] + got_far[g, rows, :].astype(F32)
            else:
                out = got_pair[g, rows, :].astype(F32) + got_other[g, rows, :].astype(F32)
            gout[same, g, rows, :] = out.astype(BF16)
        d = yl if same else 1 - yl
        start = pl.multiple_of((z * 2 + d) * ROWS + j * TILE, TILE)
        for k, dev in z_devs:
            remote(gout.at[same, (z + k) % 4, rows], tgrad_out.at[pl.ds(start, TILE)], o_s, o_r, dev).start()

    PART = HALF // PARTS
    far, summed = {}, {}
    for n in range(PARTS):
        for side, (relay, got, dev) in enumerate(((relay_l, got_l, right), (relay_r, got_r, left))):
            rows = pl.ds(side * HALF + n * PART, PART)
            far[n, side] = remote(
                send_x.at[2, rows], relay.at[pl.ds(n * PART, PART)], x2s, x2r.at[2 + 2 * n + side], dev
            )
            summed[n, side] = remote(
                send_x.at[1 - side, rows], got.at[rows], x2s, x2r.at[2 + 2 * (PARTS + n) + side], dev
            )

    def send_far():
        send_x[2] = image_sums(3).astype(BF16)
        for cp in far.values():
            cp.start()

    def combine(n):
        for side, relay in enumerate((relay_l, relay_r)):
            rows = pl.ds(side * HALF + n * PART, PART)
            far[n, side].wait_recv()
            send_x[1 - side, rows, :] = (
                send_x[1 - side, rows, :].astype(F32) + relay[pl.ds(n * PART, PART), :].astype(F32)
            ).astype(BF16)
            summed[n, side].start()

    weights((1,), 3, 1)
    text_sums(1)
    weights((2, 3), 0, 1)
    weights((3,), 3, 1)
    text_sums(3)
    project(0, 1)
    weights((0, 2, 4, 5), 3, 1)
    text_sums(0)
    project(1, 1)
    send_far()
    project(0, 0)
    weights((4, 5), 0, 1)
    text_sums(5)
    own_pairs(1)
    text_sums(2)
    project(2, 1)
    combine(0)
    feature_rows(0, 1)
    feature_rows(0, 0)
    own_pairs(2)
    text_sums(4)
    project(1, 0)
    combine(1)
    project(2, 0)
    feature_rows(1, 1)
    iacc[...] = image_sums(0)
    combine(2)
    feature_rows(1, 0)
    feature_rows(2, 1)
    feature_rows(2, 0)
    own_out = [
        pltpu.make_async_copy(
            gout.at[same, z], tgrad_out.at[own_rows(1 - yl if same == 0 else yl)], loc_sem.at[8 + same]
        )
        for same in range(2)
    ]
    for cp in own_out:
        cp.start()

    near_right.wait_recv()
    near_left.wait_recv()
    for n in range(PARTS):
        for side in range(2):
            rows = pl.ds(side * HALF + n * PART, PART)
            summed[n, side].wait_recv()
            r = irs[rows, :]
            v = iraw[rows, :].astype(F32) * r
            up = iacc[rows, :] + got_l[rows, :].astype(F32) + got_r[rows, :].astype(F32)
            d = jnp.sum(v * up, axis=-1, keepdims=True)
            igrad_out[rows, :] = (r * scale * (up - v * d)).astype(BF16)

    drain(text_hbm.at[pl.ds(0, 6 * ROWS)], zs)
    for j in range(TILES):
        drain(R.at[0, 0, pl.ds(0, 3)], ys.at[j])
    drain(R.at[0, 0, pl.ds(0, 3)], y0s)
    drain(R.at[:, :, pl.ds(0, 3)], gs)
    drain(I.at[pl.ds(0, 2 * ROWS)], cs)
    drain(I.at[pl.ds(0, 2 * ROWS)], ps)
    drain(I.at[pl.ds(0, ROWS)], xfs)
    drain(I.at[pl.ds(0, 2 * ROWS)], xs)
    drain(I.at[pl.ds(0, 3 * ROWS)], x2s)
    drain(text_hbm.at[pl.ds(0, 6 * ROWS)], o_s)
    drain(tgrad_out.at[pl.ds(0, 6 * ROWS)], o_r)
    for cp in own_out:
        cp.wait()


def write_out(a_ref, b_ref, a_out, b_out, sem):
    copies = []
    for src, dst in ((a_ref, a_out), (b_ref, b_out)):
        step = src.shape[0] // CHUNKS
        for n in range(CHUNKS):
            rows = pl.ds(n * step, step)
            copies.append(pltpu.make_async_copy(src.at[rows], dst.at[rows], sem.at[len(copies)]))
    for cp in copies:
        cp.start()
    for cp in copies:
        cp.wait()


def per_device(text_emb, image_emb, logit_scale, logit_bias, bucket, positive, blocks):
    vmem_spec = pl.BlockSpec(memory_space=pltpu.VMEM)
    hbm_spec = pl.BlockSpec(memory_space=pltpu.HBM)
    vm = pltpu.VMEM
    dma = pltpu.SemaphoreType.DMA
    tiles = bucket.shape[0] // TILE
    shapes = (
        pltpu.VMEM(text_emb.shape, BF16),
        pltpu.VMEM(image_emb.shape, BF16),
    )
    grads = pl.pallas_call(
        kernel,
        out_shape=shapes,
        in_specs=[pl.BlockSpec(memory_space=pltpu.SMEM)] * 2 + [hbm_spec] * 5,
        out_specs=(vmem_spec, vmem_spec),
        scratch_shapes=[
            vm((2, 2, 4, ROWS, EB), BF16), vm((4, ROWS, EB), BF16), vm((ROWS, E), BF16),
            vm((tiles, TILE), jnp.int32), vm((tiles, TILE), jnp.int32), vm(blocks.shape[::-1], jnp.int32),
            vm((4 * ROWS, E), BF16), vm((4 * ROWS, E), BF16), vm((4 * ROWS, 4 * ROWS), BF16), vm((4 * ROWS, 4 * ROWS), BF16),
            vm((6, 256, TILE), F32), vm((12, TILES, 16, TILE), F32),
            vm((2, ROWS, 1), F32), vm((ROWS, 1), F32),
            vm((6, TILE, E), F32), vm((ROWS, E), F32),
            vm((6, TILE, E), BF16), vm((3, ROWS, E), BF16), vm((6, TILE, E), BF16),
            vm((ROWS, E), BF16), vm((ROWS, E), BF16), vm((HALF, E), BF16), vm((HALF, E), BF16),
            vm((2, 4, ROWS, EB), F32), vm((2, 2, 4, ROWS, EB), BF16),
            vm((4, ROWS, EB), BF16), vm((4, ROWS, EB), BF16), vm((4, ROWS, EB), BF16),
            vm((2, 4, ROWS, EB), BF16),
            dma((10,)), dma, dma((3, 2)), dma, dma((2, 2)), dma, dma((2,)),
            dma, dma((3,)), dma((3,)), dma((3, 3)), dma, dma((3, 2)), dma, dma((6,)), dma, dma((3, 3)),
            dma, dma((2 + 4 * PARTS,)), dma, dma,
        ],
        compiler_params=pltpu.CompilerParams(
            collective_id=0, has_side_effects=True, vmem_limit_bytes=48 << 20
        ),
        name="pairs",
    )(
        logit_scale, logit_bias,
        *(
            pltpu.with_memory_space_constraint(a, pltpu.HBM)
            for a in (
                text_emb, image_emb,
                bucket.reshape(tiles, TILE), positive.reshape(tiles, TILE), blocks.transpose(2, 1, 0),
            )
        )
    )
    return pl.pallas_call(
        write_out,
        out_shape=(
            jax.ShapeDtypeStruct(text_emb.shape, BF16),
            jax.ShapeDtypeStruct(image_emb.shape, BF16),
        ),
        in_specs=[vmem_spec, vmem_spec],
        out_specs=(hbm_spec, hbm_spec),
        scratch_shapes=[dma((2 * CHUNKS,))],
        name="write_out",
    )(*(pltpu.with_memory_space_constraint(a, pltpu.VMEM) for a in grads))


def solution(mesh):
    in_specs = (P("blk", "tp"), P(("blk", "tp"), None), P(), P(), P(), P(), P())
    out_specs = (P("blk", "tp"), P(("blk", "tp"), None))
    return jax.shard_map(
        per_device, mesh=mesh, in_specs=in_specs, out_specs=out_specs, check_vma=False
    )
```

```python
import jax
import jax.numpy as jnp
from jax import lax
from jax.experimental import pallas as pl
from jax.experimental.pallas import tpu as pltpu
from jax.sharding import PartitionSpec as P

MESH = pl.DeviceIdType.MESH
F32 = jnp.float32
BF16 = jnp.bfloat16
TILE = 128
TILES = 3
SLOTS = 3
ROWS = TILE * TILES
HALF = ROWS // 2
CHUNKS = 4
PARTS = 3
E = 1024
GROUPS = 8
EB = E // GROUPS
LOG2E = 1.4426950408889634
NT = (((1,), (1,)), ((), ()))
NN = (((1,), (0,)), ((), ()))
TN = (((0,), (0,)), ((), ()))


def kernel(
    scale_ref, bias_ref, text_hbm, image_hbm, bucket_hbm, positive_hbm, blocks_hbm,
    tgrad_out, igrad_out,
    R, pas, iraw, bucket_v, positive_v, blocks_v,
    T, I, W, M, rowb, cnt, trs, irs,
    tacc, iacc, send_t, send_x, got_c, got_l, got_r, relay_l, relay_r,
    keep, gsend, got_far, got_pair, got_other, gout,
    loc_sem, zs, zr, xs, xr, xfs, xfr, y0s, y0r, ys, yr, cs, cr, ps, pr, gs, gr, x2s, x2r, o_s, o_r,
):
    blk = lax.axis_index("blk")
    tp = lax.axis_index("tp")
    yh = blk // 8
    x = (blk // 2) % 4
    c = blk % 2
    z = tp // 2
    yl = tp % 2
    yh_blk = (blk + 8) % 16
    tp_pair = tp + 1 - 2 * yl
    core_dev = (blk + 1 - 2 * c, tp)
    far_y = (yh_blk, tp)
    pair_y = (blk, tp_pair)
    other_y = (yh_blk, tp_pair)
    z_devs = [(k, (blk, ((z + k) % 4) * 2 + yl)) for k in range(1, 4)]
    right = ((yh * 4 + (x + 1) % 4) * 2 + c, tp)
    left = ((yh * 4 + (x + 3) % 4) * 2 + c, tp)
    far_blk = (yh * 4 + (x + 2) % 4) * 2 + c
    image_blk = (blk, left[0], right[0], far_blk)
    text_blk = ((blk, core_dev[0]), (yh_blk, yh_blk + 1 - 2 * c))

    def remote(src, dst, ssem, rsem, dev):
        return pltpu.make_async_remote_copy(
            src_ref=src, dst_ref=dst, send_sem=ssem, recv_sem=rsem,
            device_id=dev, device_id_type=MESH,
        )

    def drain(ref, sem):
        pltpu.make_async_copy(ref, ref, sem).wait()

    local = [
        pltpu.make_async_copy(image_hbm, iraw, loc_sem.at[0]),
        pltpu.make_async_copy(bucket_hbm, bucket_v, loc_sem.at[1]),
        pltpu.make_async_copy(positive_hbm, positive_v, loc_sem.at[2]),
        pltpu.make_async_copy(blocks_hbm, blocks_v, loc_sem.at[3]),
    ]
    def own_rows(d):
        return pl.ds(pl.multiple_of((z * 2 + d) * ROWS, ROWS), ROWS)

    own_text = pltpu.make_async_copy(text_hbm.at[own_rows(yl)], R.at[0, yl, z], loc_sem.at[6])
    for cp in local:
        cp.start()
    own_text.start()

    barrier = pltpu.get_barrier_semaphore()
    peers = [dev for _, dev in z_devs] + [far_y, pair_y, other_y, core_dev, right, left]
    for dev in peers:
        pl.semaphore_signal(barrier, inc=1, device_id=dev, device_id_type=MESH)

    pl.semaphore_wait(barrier, len(peers))

    def z_send(j):
        rows = pl.ds(j * TILE, TILE)
        for k, dev in z_devs:
            base = ((z + k) % 4) * 2
            for same in range(2):
                d = 1 - yl if same == 0 else yl
                start = pl.multiple_of((base + d) * ROWS + j * TILE, TILE)
                dst = R.at[0, yl, z, rows] if same else pas.at[z, rows]
                remote(text_hbm.at[pl.ds(start, TILE)], dst, zs, zr.at[j, same], dev).start()

    z_send(0)
    held = [
        remote(text_hbm.at[own_rows(1 - yl)], R.at[0, yl, z], y0s, y0r.at[0], pair_y),
        remote(text_hbm.at[own_rows(1 - yl)], R.at[1, yl, z], y0s, y0r.at[1], other_y),
        remote(text_hbm.at[own_rows(yl)], R.at[1, yl, z], y0s, y0r.at[2], far_y),
    ]
    for cp in held:
        cp.start()

    local[0].wait()
    for h in range(2):
        rows = pl.ds(h * HALF, HALF)
        v = iraw[rows, :].astype(F32)
        r = lax.rsqrt(jnp.sum(v * v, axis=-1, keepdims=True) + 1e-6)
        irs[rows, :] = r
        I[rows, :] = (v * r).astype(BF16)

    def image_send(h, side):
        return remote(
            I.at[pl.ds(h * HALF, HALF)],
            I.at[pl.ds((1 + side) * ROWS + h * HALF, HALF)],
            xs, xr.at[side, h], right if side == 0 else left,
        )

    ring = {(h, s): image_send(h, s) for h in range(2) for s in range(2)}
    ring[0, 0].start()
    ring[1, 1].start()

    for cp in local[1:]:
        cp.wait()
    scale = scale_ref[0]
    bias = bias_ref[0]
    ea = -scale * LOG2E
    eb = -bias * LOG2E

    def spread(row):
        return jnp.broadcast_to(row.astype(F32), (TILE, TILE)).T

    for side in range(2):
        for core in range(2):
            def prep(j, carry, side=side, core=core):
                r = (text_blk[side][core] * GROUPS + tp) * TILES + j
                block = 2 * j + side
                rowb[block, pl.ds(core * TILE, TILE), :] = spread(bucket_v[pl.ds(r, 1), :])
                lanes = lax.broadcasted_iota(jnp.int32, blocks_v.shape[1:], 1)
                for l in range(TILES):
                    n = sum(jnp.where(blocks_v[m] == l, 1.0, 0.0) for m in range(SLOTS))
                    n = jnp.sum(jnp.where(lanes == r, n, 0.0), axis=1, keepdims=True)
                    cnt[2 * block + core, l] = jnp.broadcast_to(n, (blocks_v.shape[1], TILE))
                return carry

            lax.fori_loop(0, TILES, prep, 0)

    z_send(1)

    def pair_masks(b, carry):
        for k in range(4):
            for l in range(TILES):
                cb = bucket_v[pl.ds((image_blk[k] * GROUPS + tp) * TILES + l, 1), :].astype(F32)
                for h in range(2):
                    rows = pl.ds(pl.multiple_of((2 * b + h) * TILE, TILE), TILE)
                    n = cnt[2 * b + h, l, pl.ds(image_blk[k], 1), :]
                    M[rows, pl.ds(k * ROWS + l * TILE, TILE)] = jnp.where(
                        rowb[b, pl.ds(h * TILE, TILE), :] == cb, n, 0.0
                    ).astype(BF16)
        return carry

    lax.fori_loop(0, 2 * TILES, pair_masks, 0)

    own_text.wait()
    along_y, to_core = [], []
    for j in range(TILES):
        rows = pl.ds(j * TILE, TILE)
        pieces = []
        for k in range(1, 4):
            zk = (z + k) % 4
            pieces += [
                remote(pas.at[zk, rows], R.at[0, yl, zk, rows], ys.at[j], yr.at[j, 0], pair_y),
                remote(pas.at[zk, rows], R.at[1, yl, zk, rows], ys.at[j], yr.at[j, 1], other_y),
                remote(R.at[0, yl, zk, rows], R.at[1, yl, zk, rows], ys.at[j], yr.at[j, 2], far_y),
            ]
        along_y.append(pieces)
        to_core.append([
            remote(T.at[pl.ds((4 * j + 2 * side) * TILE, TILE)], T.at[pl.ds((4 * j + 2 * side + 1) * TILE, TILE)], cs, cr.at[j, side], core_dev)
            for side in range(2)
        ])

    def z_ready(j):
        rows = pl.ds(j * TILE, TILE)
        drain(pas.at[pl.ds(0, 3), rows], zr.at[j, 0])
        drain(R.at[0, 0, pl.ds(0, 3), rows], zr.at[j, 1])

    def pass_on(j):
        for cp in along_y[j]:
            cp.start()

    def text_tile(j, side):
        rows = pl.ds(j * TILE, TILE)
        for kind in (0,) if side == 0 else (1, 2):
            if j == 0:
                held[kind].wait_recv()
            drain(pas.at[pl.ds(0, 3), rows], yr.at[j, kind])
        sq = jnp.zeros((TILE, EB), F32)
        for d in range(2):
            for g in range(4):
                v = R[side, d, g, rows, :].astype(F32)
                sq = sq + v * v
        r = lax.rsqrt(jnp.sum(sq, axis=-1, keepdims=True) + 1e-6)
        trs[side, rows, :] = r
        for d in range(2):
            for g in range(4):
                at = (2 * g + d) * EB
                T[pl.ds((4 * j + 2 * side) * TILE, TILE), at : at + EB] = (R[side, d, g, rows, :].astype(F32) * r).astype(BF16)
        to_core[j][side].start()

    def text_ready(j):
        for cp in to_core[j]:
            cp.wait_recv()

    z_ready(0)
    pass_on(0)
    z_send(2)
    z_ready(1)
    pass_on(1)
    ring[1, 0].start()
    ring[0, 1].start()
    z_ready(2)
    pass_on(2)
    on_right = remote(
        I.at[pl.ds(ROWS, HALF)], I.at[pl.ds(3 * ROWS, HALF)], xfs, xfr.at[0], right
    )
    on_left = remote(
        I.at[pl.ds(2 * ROWS + HALF, HALF)], I.at[pl.ds(3 * ROWS + HALF, HALF)],
        xfs, xfr.at[1], left,
    )

    def weights(blocks, k0, nk):
        cols = pl.ds(k0 * ROWS, nk * ROWS)

        for b in blocks:
            rows = pl.ds(b * 2 * TILE, 2 * TILE)
            s = lax.dot_general(T[rows, :], I[cols, :], NT, preferred_element_type=F32)
            w = pl.reciprocal(1.0 + jnp.exp2(s * ea + eb)).astype(BF16)
            W[rows, cols] = w * M[rows, cols]

    def own_pairs(j):
        at = j * TILE
        s = lax.dot_general(T[4 * at : 4 * at + TILE, :], I[at : at + TILE, :], NT, preferred_element_type=F32)
        e = jnp.exp2(s * ea + eb)
        tile = (blk * GROUPS + tp) * TILES + j
        n = cnt[4 * j, j, pl.ds(blk, 1), :]
        pos = spread(positive_v[pl.ds(tile, 1), :] - tile * TILE)
        matched = pos == lax.broadcasted_iota(jnp.int32, (TILE, TILE), 1).astype(F32)
        num = jnp.where(matched, -n * e, M[4 * at : 4 * at + TILE, at : at + TILE].astype(F32))
        W[4 * at : 4 * at + TILE, at : at + TILE] = (num / (1.0 + e)).astype(BF16)

    def image_sums(k):
        return lax.dot_general(W[:, pl.ds(k * ROWS, ROWS)], T[...], TN, preferred_element_type=F32)

    text_tile(0, 0)
    text_tile(0, 1)
    text_ready(0)
    weights((0, 1), 0, 1)
    own_pairs(0)
    ring[0, 0].wait_recv()
    on_right.start()
    ring[1, 1].wait_recv()
    on_left.start()
    text_tile(1, 0)
    text_tile(1, 1)
    text_ready(1)
    text_tile(2, 0)
    text_tile(2, 1)
    ring[1, 0].wait_recv()
    ring[0, 1].wait_recv()
    weights(range(4), 1, 2)
    text_ready(2)
    weights((4, 5), 2, 1)
    first = pl.ds(0, HALF)
    second = pl.ds(HALF, HALF)
    send_x[1] = image_sums(2).astype(BF16)
    near_right = remote(send_x.at[1, second], got_l.at[second], x2s, x2r.at[0], right)
    near_right.start()
    weights((4, 5), 1, 1)
    send_x[0] = image_sums(1).astype(BF16)
    near_left = remote(send_x.at[0, first], got_r.at[first], x2s, x2r.at[1], left)
    near_left.start()
    on_right.wait_recv()
    on_left.wait_recv()
    partial = [
        remote(send_t.at[b], got_c.at[b], ps, pr.at[b], core_dev) for b in range(2 * TILES)
    ]

    def text_sums(b):
        u = lax.dot_general(W[pl.ds(b * 2 * TILE, 2 * TILE), :], I[...], NN, preferred_element_type=F32)
        tacc[b] = u[0:TILE]
        send_t[b] = u[TILE:].astype(BF16)
        partial[b].start()

    back = []
    for j in range(TILES):
        rows = pl.ds(j * TILE, TILE)
        back.append([
            remote(gsend.at[0, 1 - yl, :, rows], got_pair.at[:, rows], gs, gr.at[j, 0], pair_y),
            remote(gsend.at[1, 1 - yl, :, rows], got_other.at[:, rows], gs, gr.at[j, 1], other_y),
            remote(gsend.at[1, yl, :, rows], got_far.at[:, rows], gs, gr.at[j, 2], far_y),
        ])

    def project(j, side):
        b = 2 * j + side
        rows = pl.ds(j * TILE, TILE)
        partial[b].wait_recv()
        r = trs[side, rows, :]
        rs = r * scale
        up = tacc[b] + got_c[b].astype(F32)
        dot = jnp.zeros((TILE, EB), F32)
        for d in range(2):
            for g in range(4):
                at = (2 * g + d) * EB
                dot = dot + R[side, d, g, rows, :].astype(F32) * r * up[:, at : at + EB]
        total = jnp.sum(dot, axis=-1, keepdims=True)
        for d in range(2):
            for g in range(4):
                at = (2 * g + d) * EB
                u = R[side, d, g, rows, :].astype(F32) * r
                out = rs * (up[:, at : at + EB] - u * total)
                gsend[side, d, g, rows, :] = out.astype(BF16)
                if side == 0:
                    keep[d, g, rows, :] = out
        if side == 0:
            back[j][0].start()
        else:
            back[j][1].start()
            back[j][2].start()

    def feature_rows(j, same):
        rows = pl.ds(j * TILE, TILE)
        for cp in back[j][2:] if same else back[j][:2]:
            cp.wait_recv()
        for g in range(4):
            if same:
                out = keep[yl, g, rows, :] + got_far[g, rows, :].astype(F32)
            else:
                out = got_pair[g, rows, :].astype(F32) + got_other[g, rows, :].astype(F32)
            gout[same, g, rows, :] = out.astype(BF16)
        d = yl if same else 1 - yl
        start = pl.multiple_of((z * 2 + d) * ROWS + j * TILE, TILE)
        for k, dev in z_devs:
            remote(gout.at[same, (z + k) % 4, rows], tgrad_out.at[pl.ds(start, TILE)], o_s, o_r, dev).start()

    PART = HALF // PARTS
    far, summed = {}, {}
    for n in range(PARTS):
        for side, (relay, got, dev) in enumerate(((relay_l, got_l, right), (relay_r, got_r, left))):
            rows = pl.ds(side * HALF + n * PART, PART)
            far[n, side] = remote(
                send_x.at[2, rows], relay.at[pl.ds(n * PART, PART)], x2s, x2r.at[2 + 2 * n + side], dev
            )
            summed[n, side] = remote(
                send_x.at[1 - side, rows], got.at[rows], x2s, x2r.at[2 + 2 * (PARTS + n) + side], dev
            )

    def send_far():
        send_x[2] = image_sums(3).astype(BF16)
        for cp in far.values():
            cp.start()

    def combine(n):
        for side, relay in enumerate((relay_l, relay_r)):
            rows = pl.ds(side * HALF + n * PART, PART)
            far[n, side].wait_recv()
            send_x[1 - side, rows, :] = (
                send_x[1 - side, rows, :].astype(F32) + relay[pl.ds(n * PART, PART), :].astype(F32)
            ).astype(BF16)
            summed[n, side].start()

    weights((1,), 3, 1)
    text_sums(1)
    weights((2, 3), 0, 1)
    weights((3,), 3, 1)
    text_sums(3)
    project(0, 1)
    weights((0, 2, 4, 5), 3, 1)
    text_sums(0)
    project(1, 1)
    send_far()
    project(0, 0)
    weights((4, 5), 0, 1)
    text_sums(5)
    own_pairs(1)
    text_sums(2)
    project(2, 1)
    combine(0)
    feature_rows(0, 1)
    feature_rows(0, 0)
    own_pairs(2)
    text_sums(4)
    project(1, 0)
    combine(1)
    project(2, 0)
    feature_rows(1, 1)
    iacc[...] = image_sums(0)
    combine(2)
    feature_rows(1, 0)
    feature_rows(2, 1)
    feature_rows(2, 0)
    own_out = [
        pltpu.make_async_copy(
            gout.at[same, z], tgrad_out.at[own_rows(1 - yl if same == 0 else yl)], loc_sem.at[8 + same]
        )
        for same in range(2)
    ]
    for cp in own_out:
        cp.start()

    near_right.wait_recv()
    near_left.wait_recv()
    for n in range(PARTS):
        for side in range(2):
            rows = pl.ds(side * HALF + n * PART, PART)
            summed[n, side].wait_recv()
            r = irs[rows, :]
            v = iraw[rows, :].astype(F32) * r
            up = iacc[rows, :] + got_l[rows, :].astype(F32) + got_r[rows, :].astype(F32)
            d = jnp.sum(v * up, axis=-1, keepdims=True)
            igrad_out[rows, :] = (r * scale * (up - v * d)).astype(BF16)

    drain(text_hbm.at[pl.ds(0, 6 * ROWS)], zs)
    for j in range(TILES):
        drain(R.at[0, 0, pl.ds(0, 3)], ys.at[j])
    drain(R.at[0, 0, pl.ds(0, 3)], y0s)
    drain(R.at[:, :, pl.ds(0, 3)], gs)
    drain(I.at[pl.ds(0, 2 * ROWS)], cs)
    drain(I.at[pl.ds(0, 2 * ROWS)], ps)
    drain(I.at[pl.ds(0, ROWS)], xfs)
    drain(I.at[pl.ds(0, 2 * ROWS)], xs)
    drain(I.at[pl.ds(0, 3 * ROWS)], x2s)
    drain(text_hbm.at[pl.ds(0, 6 * ROWS)], o_s)
    drain(tgrad_out.at[pl.ds(0, 6 * ROWS)], o_r)
    for cp in own_out:
        cp.wait()


def write_out(a_ref, b_ref, a_out, b_out, sem):
    copies = []
    for src, dst in ((a_ref, a_out), (b_ref, b_out)):
        step = src.shape[0] // CHUNKS
        for n in range(CHUNKS):
            rows = pl.ds(n * step, step)
            copies.append(pltpu.make_async_copy(src.at[rows], dst.at[rows], sem.at[len(copies)]))
    for cp in copies:
        cp.start()
    for cp in copies:
        cp.wait()


def per_device(text_emb, image_emb, logit_scale, logit_bias, bucket, positive, blocks):
    vmem_spec = pl.BlockSpec(memory_space=pltpu.VMEM)
    hbm_spec = pl.BlockSpec(memory_space=pltpu.HBM)
    vm = pltpu.VMEM
    dma = pltpu.SemaphoreType.DMA
    tiles = bucket.shape[0] // TILE
    shapes = (
        pltpu.VMEM(text_emb.shape, BF16),
        pltpu.VMEM(image_emb.shape, BF16),
    )
    grads = pl.pallas_call(
        kernel,
        out_shape=shapes,
        in_specs=[pl.BlockSpec(memory_space=pltpu.SMEM)] * 2 + [hbm_spec] * 5,
        out_specs=(vmem_spec, vmem_spec),
        scratch_shapes=[
            vm((2, 2, 4, ROWS, EB), BF16), vm((4, ROWS, EB), BF16), vm((ROWS, E), BF16),
            vm((tiles, TILE), jnp.int32), vm((tiles, TILE), jnp.int32), vm(blocks.shape[::-1], jnp.int32),
            vm((4 * ROWS, E), BF16), vm((4 * ROWS, E), BF16), vm((4 * ROWS, 4 * ROWS), BF16), vm((4 * ROWS, 4 * ROWS), BF16),
            vm((6, 256, TILE), F32), vm((12, TILES, 16, TILE), F32),
            vm((2, ROWS, 1), F32), vm((ROWS, 1), F32),
            vm((6, TILE, E), F32), vm((ROWS, E), F32),
            vm((6, TILE, E), BF16), vm((3, ROWS, E), BF16), vm((6, TILE, E), BF16),
            vm((ROWS, E), BF16), vm((ROWS, E), BF16), vm((HALF, E), BF16), vm((HALF, E), BF16),
            vm((2, 4, ROWS, EB), F32), vm((2, 2, 4, ROWS, EB), BF16),
            vm((4, ROWS, EB), BF16), vm((4, ROWS, EB), BF16), vm((4, ROWS, EB), BF16),
            vm((2, 4, ROWS, EB), BF16),
            dma((10,)), dma, dma((3, 2)), dma, dma((2, 2)), dma, dma((2,)),
            dma, dma((3,)), dma((3,)), dma((3, 3)), dma, dma((3, 2)), dma, dma((6,)), dma, dma((3, 3)),
            dma, dma((2 + 4 * PARTS,)), dma, dma,
        ],
        compiler_params=pltpu.CompilerParams(
            collective_id=0, has_side_effects=True, vmem_limit_bytes=48 << 20
        ),
        name="pairs",
    )(
        logit_scale, logit_bias,
        *(
            pltpu.with_memory_space_constraint(a, pltpu.HBM)
            for a in (
                text_emb, image_emb,
                bucket.reshape(tiles, TILE), positive.reshape(tiles, TILE), blocks.transpose(2, 1, 0),
            )
        )
    )
    return pl.pallas_call(
        write_out,
        out_shape=(
            jax.ShapeDtypeStruct(text_emb.shape, BF16),
            jax.ShapeDtypeStruct(image_emb.shape, BF16),
        ),
        in_specs=[vmem_spec, vmem_spec],
        out_specs=(hbm_spec, hbm_spec),
        scratch_shapes=[dma((2 * CHUNKS,))],
        name="write_out",
    )(*(pltpu.with_memory_space_constraint(a, pltpu.VMEM) for a in grads))


def solution(mesh):
    in_specs = (P("blk", "tp"), P(("blk", "tp"), None), P(), P(), P(), P(), P())
    out_specs = (P("blk", "tp"), P(("blk", "tp"), None))
    return jax.shard_map(
        per_device, mesh=mesh, in_specs=in_specs, out_specs=out_specs, check_vma=False
    )
```
